32 devices in a mesh: win: 2 (over y), row: 16 (over z, x, core).
Axes of the slice: x: 2, y: 2, z: 4, core: 2. Of those that a mesh axis runs over, the one named last changes fastest.
Arguments:
- raw: bfloat16 [4096, 16384], P(None, ('win', 'row')), parts along dimension 1, may hold values from -30 to 30, as said below
- fir_taps: float32 [16], replicated, may hold values from -1.5 to 1.5
- band_width: int32 [16], P('row'), may hold values from 1 to 8, as said below
- dead_count: int32 [16], P('row'), may hold values from 0 to 64, as said below
Outputs:
- correlations: bfloat16 [8192, 8, 8, 256], P(('win', 'row')), parts along dimension 0
The draws below stay inside these ranges and needn't reach their ends.
There are 2 independent parts, one for each index of `win`. The reference program is written for one: setup_inputs(seed, part) draws one part's arguments, and reference() takes and returns one part's arrays. A program takes and returns all parts, laid end to end along the dimension named above; an argument that names none is the same for every part. Nothing has to cross between parts.
Inputs may be any that keep to these rules, and one draw needn't show every extreme that they name: `raw`: samples of the record. Row tile t pairs with column tiles t to t + band_width[t] - 1; band_width[t] <= 16 - t, and tile 0 pairs with 8 tiles. `dead_count`: some tile has 64 dead channels.
All inputs are finite; a program needn't handle non-finite values.
Results may differ from the reference program's by a relative error of at most 0.0069.
Values may be sent and summed in bfloat16 or wider, within the bound.
No kernel may reach another device: no remote copies, remote signals or barrier semaphores. Data moves between devices by JAX's collectives and lax.ppermute only.
A program may use at most 128 MiB of HBM per device.

```python
import math
import jax
import jax.numpy as jnp
from jax import lax

CH = 256
NT = 2048
NF = 512
DEC = 4
TAPS = 16
SMOOTH = 64
LAGS = 8
NB = 8
NTILE = 16
CHANNELS = 4096
RAW = 8192


def draw_raw(key, part):
    key_gain, key_noise = jax.random.split(key, 2)
    gains = jnp.exp(jax.random.uniform(key_gain, (CHANNELS, 1), jnp.float32, 0.0, math.log(10.0)))
    values = gains * jax.random.normal(key_noise, (CHANNELS, RAW), jnp.float32)
    return jnp.clip(values, -30.0, 30.0).astype(jnp.bfloat16)


def draw_band_width(key, part):
    widths = jax.random.randint(key, (NTILE,), 1, NB + 1, dtype=jnp.int32)
    positions = jnp.arange(NTILE, dtype=jnp.int32)
    widths = jnp.minimum(widths, NTILE - positions)
    return jnp.where(positions == 0, NB, widths).astype(jnp.int32)


def draw_dead_count(key, part):
    counts = jax.random.randint(key, (NTILE,), 0, CH // 4 + 1, dtype=jnp.int32)
    positions = jnp.arange(NTILE, dtype=jnp.int32)
    return jnp.where(positions == 1, CH // 4, counts).astype(jnp.int32)


def normal_values(key, shape, spread, reach, held_as=jnp.bfloat16):
    values = jax.random.normal(key, shape, jnp.float32) * spread
    return jnp.minimum(jnp.maximum(values, -reach), reach).astype(held_as)


def setup_inputs(seed: int = 0, part: int = 0) -> dict:
    splits = jax.random.split(jax.random.key(seed), 5)
    own_keys = jax.random.split(jax.random.fold_in(splits[4], part), 5)
    return {
        "raw": draw_raw(jax.random.fold_in(jax.random.fold_in(splits[4], part), 71), part),
        "fir_taps": normal_values(splits[1], (TAPS,), TAPS ** -0.5, 1.5, jnp.float32),
        "band_width": draw_band_width(jax.random.fold_in(splits[4], 71), part),
        "dead_count": draw_dead_count(jax.random.fold_in(splits[4], 71), part),
    }


def fir_decimate(padded, fir_taps, count):
    left_reach = (TAPS - DEC) // 2
    filtered = jnp.zeros((padded.shape[0], count), jnp.float32)
    for tap_index in range(TAPS):
        first_at = 2 * DEC - left_reach + tap_index
        sampled = lax.slice_in_dim(padded, first_at, first_at + (count - 1) * DEC + 1, DEC, 1)
        filtered = filtered + fir_taps[tap_index] * sampled
    return filtered

def spectral_table():
    sample_ids = jnp.arange(NT, dtype=jnp.int32)[:, None]
    bin_ids = jnp.arange(NF, dtype=jnp.int32)[None, :] + 1
    phases = (sample_ids * bin_ids % NT).astype(jnp.float32) * (2.0 * math.pi / NT)
    return jnp.concatenate([jnp.cos(phases), -jnp.sin(phases)], axis=1).astype(jnp.bfloat16)

def whiten(decimated):
    spectrum = jnp.dot(decimated, spectral_table(), preferred_element_type=jnp.float32)
    real_part = spectrum[:, :NF]
    imag_part = spectrum[:, NF:]
    power_bins = real_part * real_part + imag_part * imag_part
    bin_ids = jnp.arange(NF, dtype=jnp.int32)
    window = (jnp.abs(bin_ids[:, None] - bin_ids[None, :]) <= SMOOTH).astype(jnp.float32)
    counts = lax.optimization_barrier(jnp.sum(window, axis=0))
    smoothed = jnp.dot(power_bins, window, precision=lax.Precision.HIGHEST, preferred_element_type=jnp.float32) / counts
    factor = lax.rsqrt(smoothed + 1e-05)
    return (real_part * factor, imag_part * factor)

def lag_rows(white_real, white_imag):
    lag_ids = jnp.arange(LAGS, dtype=jnp.int32) - LAGS // 2
    bin_ids = jnp.arange(NF, dtype=jnp.int32) + 1
    phases = ((lag_ids % NT)[:, None] * bin_ids[None, :] % NT).astype(jnp.float32) * (2.0 * math.pi / NT)
    cosine_table = jnp.cos(phases)[None]
    sine_table = jnp.sin(phases)[None]
    rotated_real = white_real[:, None, :] * cosine_table - white_imag[:, None, :] * sine_table
    rotated_imag = white_real[:, None, :] * sine_table + white_imag[:, None, :] * cosine_table
    stacked = jnp.concatenate([rotated_real, rotated_imag], axis=2).astype(jnp.bfloat16)
    return stacked.reshape(-1, 2 * NF)

def correlate(lagged, column_tile, keep_flag):
    product = lax.dot_general(lagged, column_tile, (((1,), (1,)), ((), ())), preferred_element_type=jnp.float32)
    return product * (keep_flag / math.sqrt(NF))

def reference(raw, fir_taps, band_width, dead_count):

    def prepare(operands):
        tile_raw, tile_dead = operands
        padded = jnp.pad(tile_raw.astype(jnp.float32), ((0, 0), (2 * DEC, 2 * DEC)))
        filtered = fir_decimate(padded, fir_taps, NT)
        keep_mask = (jnp.arange(CH, dtype=jnp.int32) >= tile_dead).astype(jnp.float32)[:, None]
        decimated = (filtered * keep_mask).astype(jnp.bfloat16)
        white_real, white_imag = whiten(decimated)
        white = jnp.concatenate([white_real, white_imag], axis=1).astype(jnp.bfloat16)
        return (white, lag_rows(white_real, white_imag))
    whites, lagged_all = lax.map(prepare, (raw.reshape(NTILE, CH, RAW), dead_count))

    def pair_row(operands):
        lagged, band_span, tile_index = operands
        blocks = []
        for offset in range(NB):
            column_tile = whites[jnp.minimum(tile_index + offset, NTILE - 1)]
            keep_flag = (offset < band_span).astype(jnp.float32)
            blocks.append(correlate(lagged, column_tile, keep_flag).reshape(CH, LAGS, CH))
        return jnp.stack(blocks, axis=2).astype(jnp.bfloat16)
    result = lax.map(pair_row, (lagged_all, band_width, jnp.arange(NTILE, dtype=jnp.int32)))
    return result.reshape(CHANNELS, LAGS, NB, CH)
```

```python
import functools
import math

import jax
import jax.numpy as jnp
import ml_dtypes
import numpy as np
from jax import lax
from jax.experimental import pallas as pl
from jax.experimental.pallas import tpu as pltpu
from jax.sharding import PartitionSpec as P

NT = 2048
NF = 512
DEC = 4
TAPS = 16
SMOOTH = 64
LAGS = 8
NB = 8
LEFT = (TAPS - DEC) // 2
LANES = 128
EDGE = 8
PLANE = 4
FLOAT = jnp.float32
HALF = jnp.bfloat16


def table_rows(samples):
    bins = np.arange(NF, dtype=np.int64)[None, :] + 1
    samples = np.asarray(samples, dtype=np.int64)[:, None]
    phases = (samples * bins % NT).astype(np.float64) * (2.0 * math.pi / NT)
    rows = np.concatenate([np.cos(phases), -np.sin(phases)], axis=1)
    inside = (samples >= 0) & (samples < NT)
    return np.where(inside, rows, 0.0).astype(ml_dtypes.bfloat16)


def edge_samples():
    blocks = NT // LANES
    offsets = np.array([-2, -1, LANES, LANES + 1] * 2)
    return (np.arange(blocks)[:, None] * LANES + offsets[None, :]).reshape(-1)


def window_table():
    ids = np.arange(NF)
    window = np.abs(ids[:, None] - ids[None, :]) <= SMOOTH
    counts = window.sum(axis=0).astype(np.float32)[None, :]
    return window.astype(ml_dtypes.bfloat16), counts


def lag_tables():
    lags = np.arange(LAGS, dtype=np.int64) - LAGS // 2
    bins = np.arange(NF, dtype=np.int64) + 1
    phases = ((lags % NT)[:, None] * bins[None, :] % NT) * (2.0 * math.pi / NT)
    return np.cos(phases).astype(np.float32), np.sin(phases).astype(np.float32)


def split(value):
    high = value.astype(HALF)
    low = (value - high.astype(FLOAT)).astype(HALF)
    return high, low


def spread_taps(taps, index):
    spread = jnp.zeros(index.shape, FLOAT)
    for tap in range(TAPS):
        spread = jnp.where(index == tap, taps[tap], spread)
    return spread


def filter_body(taps, raw, out, main, edge, *, channels):
    width = raw.shape[1]

    @pl.when(pl.program_id(0) == 0)
    def _():
        rows = lax.broadcasted_iota(jnp.int32, (width, LANES), 0)
        cols = lax.broadcasted_iota(jnp.int32, (width, LANES), 1)
        high, low = split(spread_taps(taps, rows - DEC * cols + LEFT))
        main[:, :LANES] = high
        main[:, LANES:] = low
        row = lax.broadcasted_iota(jnp.int32, (EDGE, 2 * LANES), 0) % 4
        lane = lax.broadcasted_iota(jnp.int32, (EDGE, 2 * LANES), 1)
        lane = jnp.where(lane < LANES, lane, lane + width - 2 * LANES)
        sample = jnp.where(row < 2, row - 2, row + LANES - 2)
        high, low = split(spread_taps(taps, lane - DEC * sample + LEFT))
        edge[...] = jnp.concatenate([high.astype(FLOAT), low.astype(FLOAT)], axis=0).astype(HALF)

    for tile in range(out.shape[0]):
        block = raw[pl.ds(tile * channels, channels), :]
        product = jnp.dot(block, main[...], preferred_element_type=FLOAT)
        out[tile, :channels, :] = (product[:, :LANES] + product[:, LANES:]).astype(HALF)
        ends = jnp.concatenate([block[:, :LANES], block[:, width - LANES :]], axis=1)
        partial = lax.dot_general(
            edge[...], ends, (((1,), (1,)), ((), ())), preferred_element_type=FLOAT
        )
        partial = partial[:EDGE] + partial[EDGE:]
        row = lax.broadcasted_iota(jnp.int32, (EDGE, LANES), 0)
        picked = jnp.where(row < 4, partial[:, :LANES], partial[:, LANES:])
        out[tile, channels:, :] = picked.astype(HALF)


def filter_blocks(raw, fir_taps, tiles):
    channels = raw.shape[0] // tiles
    width = raw.shape[1]
    step = 2
    return pl.pallas_call(
        functools.partial(filter_body, channels=channels),
        out_shape=jax.ShapeDtypeStruct((tiles, channels + EDGE, LANES), HALF),
        grid=(tiles // step,),
        in_specs=[
            pl.BlockSpec(memory_space=pltpu.SMEM),
            pl.BlockSpec((step * channels, width), lambda i: (i, 0)),
        ],
        out_specs=pl.BlockSpec((step, channels + EDGE, LANES), lambda i: (i, 0, 0)),
        scratch_shapes=[
            pltpu.VMEM((width, 2 * LANES), HALF),
            pltpu.VMEM((2 * EDGE, 2 * LANES), HALF),
        ],
        compiler_params=pltpu.CompilerParams(vmem_limit_bytes=16 << 20),
        name="filter",
    )(fir_taps, raw)


def filter_whole(channel_block, fir_taps):
    padded = jnp.pad(channel_block.astype(FLOAT), ((0, 0), (2 * DEC, 2 * DEC)))
    rows = padded.shape[0]
    phased = jnp.transpose(padded.reshape(rows, -1, DEC), (2, 0, 1))
    filtered = jnp.zeros((rows, NT), FLOAT)
    for tap in range(TAPS):
        first_at = 2 * DEC - LEFT + tap
        begin = first_at // DEC
        filtered = filtered + fir_taps[tap] * phased[first_at % DEC, :, begin : begin + NT]
    blocks = filtered.astype(HALF).reshape(rows, NT // LANES, LANES).transpose(1, 0, 2)
    return jnp.concatenate([blocks, jnp.zeros((NT // LANES, EDGE, LANES), HALF)], axis=1)


def whiten_body(dead, blocks, table, edge_table, window, counts, white, real, imag, total, ends):
    step = pl.program_id(0)
    group = blocks.shape[0]
    channels = white.shape[0]
    left = jnp.concatenate([blocks[i, :channels, :] for i in range(group)], axis=1)
    part = jnp.dot(left, table[...], preferred_element_type=FLOAT)
    for i in range(group):
        at = pl.multiple_of((step * group + i) * EDGE, EDGE)
        ends[pl.ds(at, EDGE), :] = blocks[i, channels:, :].astype(FLOAT)

    @pl.when(step == 0)
    def _():
        total[...] = part

    @pl.when(step > 0)
    def _():
        total[...] += part

    @pl.when(step == pl.num_programs(0) - 1)
    def _():
        turned = ends[...].T
        lane = lax.broadcasted_iota(jnp.int32, turned.shape, 1) % EDGE
        first = jnp.where(lane < 4, turned, 0.0)
        second = jnp.where(lane < 4, 0.0, turned)
        edges = jnp.concatenate([first, second], axis=0).astype(HALF)
        spectrum = total[...] + jnp.dot(edges, edge_table[...], preferred_element_type=FLOAT)
        channel = lax.broadcasted_iota(jnp.int32, spectrum.shape, 0)
        spectrum = jnp.where(channel < dead[0], 0.0, spectrum)
        re, im = spectrum[:, :NF], spectrum[:, NF:]
        high, low = split(re * re + im * im)
        summed = jnp.dot(high, window[...], preferred_element_type=FLOAT)
        summed += jnp.dot(low, window[...], preferred_element_type=FLOAT)
        factor = lax.rsqrt(summed / counts[...] + 1e-05)
        re, im = re * factor, im * factor
        real[...] = re
        imag[...] = im
        white[:, :NF] = re.astype(HALF)
        white[:, NF:] = im.astype(HALF)


def whiten(blocks, dead):
    count, height, _ = blocks.shape
    channels = height - EDGE
    group = 4
    window, counts = window_table()
    return pl.pallas_call(
        whiten_body,
        out_shape=(
            jax.ShapeDtypeStruct((channels, 2 * NF), HALF),
            jax.ShapeDtypeStruct((channels, NF), FLOAT),
            jax.ShapeDtypeStruct((channels, NF), FLOAT),
        ),
        grid=(count // group,),
        in_specs=[
            pl.BlockSpec(memory_space=pltpu.SMEM),
            pl.BlockSpec((group, height, LANES), lambda i: (i, 0, 0)),
            pl.BlockSpec((group * LANES, 2 * NF), lambda i: (i, 0)),
            pl.BlockSpec((count * EDGE, 2 * NF), lambda i: (0, 0)),
            pl.BlockSpec((NF, NF), lambda i: (0, 0)),
            pl.BlockSpec((1, NF), lambda i: (0, 0)),
        ],
        out_specs=(
            pl.BlockSpec((channels, 2 * NF), lambda i: (0, 0)),
            pl.BlockSpec((channels, NF), lambda i: (0, 0)),
            pl.BlockSpec((channels, NF), lambda i: (0, 0)),
        ),
        scratch_shapes=[
            pltpu.VMEM((channels, 2 * NF), FLOAT),
            pltpu.VMEM((count * EDGE, LANES), FLOAT),
        ],
        compiler_params=pltpu.CompilerParams(vmem_limit_bytes=32 << 20),
        name="whiten",
    )(
        dead,
        blocks,
        jnp.asarray(table_rows(np.arange(NT))),
        jnp.asarray(table_rows(edge_samples())),
        jnp.asarray(window),
        jnp.asarray(counts),
    )


def send(value, target, keep=lambda source: True):
    count = lax.axis_size("row")
    pairs = [(s, target(s)) for s in range(count) if keep(s) and 0 <= target(s) < count]
    return lax.ppermute(value, "row", pairs)


def gather_band(white):
    planes = [white]
    planes.append(send(white, lambda s: s - PLANE))
    planes.append(send(planes[1], lambda s: s - PLANE, lambda s: s % PLANE != 3))
    across = [
        send(planes[0], lambda s: s ^ 2, lambda s: s & 2 == 2),
        send(planes[1], lambda s: s ^ 2),
        send(planes[2], lambda s: s ^ 2, lambda s: s & 2 == 0),
    ]
    beside = [send(plane, lambda s: s ^ 1) for plane in planes]
    corner = [
        send(across[0], lambda s: s ^ 1, lambda s: s & 2 == 0),
        send(across[1], lambda s: s ^ 1),
        send(across[2], lambda s: s ^ 1, lambda s: s & 2 == 2),
    ]
    return [[planes[p], beside[p], across[p], corner[p]] for p in range(3)]


def correlate_body(place, real, imag, cosine, sine, *rest, rows):
    band, out, columns, lagged, wide, sems = rest[:12], rest[12], *rest[13:]
    channels = columns.shape[1]

    @pl.when(pl.program_id(0) == 0)
    def _():
        for offset in range(NB):
            for at in range(PLANE):
                plane, index = divmod(at + offset, PLANE)

                @pl.when(place[0] == at)
                def _():
                    source = band[plane * PLANE + (at ^ index)]
                    pltpu.make_async_copy(source, columns.at[offset], sems.at[offset]).start()

        for offset in range(NB):
            pltpu.make_async_copy(band[0], columns.at[offset], sems.at[offset]).wait()

    re, im = real[...], imag[...]
    for lag in range(LAGS):
        c, s = cosine[lag : lag + 1, :], sine[lag : lag + 1, :]
        lagged[pl.ds(lag * rows, rows), :NF] = (re * c - im * s).astype(HALF)
        lagged[pl.ds(lag * rows, rows), NF:] = (re * s + im * c).astype(HALF)
    for offset in range(NB):
        scale = jnp.where(offset < place[1], 1.0 / math.sqrt(NF), 0.0)
        product = lax.dot_general(
            lagged[...], columns[offset], (((1,), (1,)), ((), ())), preferred_element_type=FLOAT
        )
        product = product * scale
        for lag in range(LAGS):
            part = product[lag * rows : (lag + 1) * rows]
            for half in range(channels // LANES):
                columns_at = slice(half * LANES, (half + 1) * LANES)
                wide[half, pl.ds(lag * NB + offset, rows, LAGS * NB), :] = part[:, columns_at]
    for half in range(channels // LANES):
        block = wide[half].reshape(rows, LAGS, NB, LANES)
        out[:, :, :, half * LANES : (half + 1) * LANES] = block.astype(HALF)


def correlate(real, imag, band, place):
    channels = real.shape[0]
    rows = 32
    cosine, sine = lag_tables()
    flat = [tile for plane in band for tile in plane]
    return pl.pallas_call(
        functools.partial(correlate_body, rows=rows),
        out_shape=jax.ShapeDtypeStruct((channels, LAGS, NB, channels), HALF),
        grid=(channels // rows,),
        in_specs=[
            pl.BlockSpec(memory_space=pltpu.SMEM),
            pl.BlockSpec((rows, NF), lambda i: (i, 0)),
            pl.BlockSpec((rows, NF), lambda i: (i, 0)),
            pl.BlockSpec((LAGS, NF), lambda i: (0, 0)),
            pl.BlockSpec((LAGS, NF), lambda i: (0, 0)),
        ]
        + [pl.BlockSpec(memory_space=pl.ANY)] * len(flat),
        out_specs=pl.BlockSpec((rows, LAGS, NB, channels), lambda i: (i, 0, 0, 0)),
        scratch_shapes=[
            pltpu.VMEM((NB, channels, 2 * NF), HALF),
            pltpu.VMEM((LAGS * rows, 2 * NF), HALF),
            pltpu.VMEM((channels // LANES, rows * LAGS * NB, LANES), FLOAT),
            pltpu.SemaphoreType.DMA((NB,)),
        ],
        compiler_params=pltpu.CompilerParams(vmem_limit_bytes=32 << 20),
        name="correlate",
    )(place, real, imag, jnp.asarray(cosine), jnp.asarray(sine), *flat)


def shards(raw, fir_taps, band_width, dead_count):
    tiles = lax.axis_size("row")
    if raw.shape[1] == DEC * LANES:
        blocks = filter_blocks(raw, fir_taps, tiles)
        blocks = lax.all_to_all(blocks, "row", split_axis=0, concat_axis=0, tiled=True)
    else:
        channel_block = lax.all_to_all(raw, "row", split_axis=0, concat_axis=1, tiled=True)
        blocks = filter_whole(channel_block, fir_taps)
    white, real, imag = whiten(blocks, dead_count)
    band = gather_band(white)
    place = jnp.stack([lax.axis_index("row").astype(jnp.int32) % PLANE, band_width[0]])
    return correlate(real, imag, band, place)


def solution(mesh):
    return jax.shard_map(
        shards,
        mesh=mesh,
        in_specs=(P(None, ("win", "row")), P(), P("row"), P("row")),
        out_specs=P(("win", "row"), None, None, None),
        check_vma=False,
    )
```

```python
import functools
import math

import jax
import jax.numpy as jnp
import ml_dtypes
import numpy as np
from jax import lax
from jax.experimental import pallas as pl
from jax.experimental.pallas import tpu as pltpu
from jax.sharding import PartitionSpec as P

NT = 2048
NF = 512
DEC = 4
TAPS = 16
SMOOTH = 64
LAGS = 8
NB = 8
LEFT = (TAPS - DEC) // 2
LANES = 128
EDGE = 8
FLOAT = jnp.float32
HALF = jnp.bfloat16


def table_rows(samples):
    bins = np.arange(NF, dtype=np.int64)[None, :] + 1
    samples = np.asarray(samples, dtype=np.int64)[:, None]
    phases = (samples * bins % NT).astype(np.float64) * (2.0 * math.pi / NT)
    rows = np.concatenate([np.cos(phases), -np.sin(phases)], axis=1)
    inside = (samples >= 0) & (samples < NT)
    return np.where(inside, rows, 0.0).astype(ml_dtypes.bfloat16)


def edge_samples():
    blocks = NT // LANES
    offsets = np.array([-2, -1, LANES, LANES + 1] * 2)
    return (np.arange(blocks)[:, None] * LANES + offsets[None, :]).reshape(-1)


def window_table():
    ids = np.arange(NF)
    window = np.abs(ids[:, None] - ids[None, :]) <= SMOOTH
    counts = window.sum(axis=0).astype(np.float32)[None, :]
    return window.astype(ml_dtypes.bfloat16), counts


def lag_tables():
    lags = np.arange(LAGS, dtype=np.int64) - LAGS // 2
    bins = np.arange(NF, dtype=np.int64) + 1
    phases = ((lags % NT)[:, None] * bins[None, :] % NT) * (2.0 * math.pi / NT)
    return np.cos(phases).astype(np.float32), np.sin(phases).astype(np.float32)


def split(value):
    high = value.astype(HALF)
    low = (value - high.astype(FLOAT)).astype(HALF)
    return high, low


def spread_taps(taps, index):
    spread = jnp.zeros(index.shape, FLOAT)
    for tap in range(TAPS):
        spread = jnp.where(index == tap, taps[tap], spread)
    return spread


def filter_body(taps, raw, out, main, edge, *, channels):
    width = raw.shape[1]

    @pl.when(pl.program_id(0) == 0)
    def _():
        rows = lax.broadcasted_iota(jnp.int32, (width, LANES), 0)
        cols = lax.broadcasted_iota(jnp.int32, (width, LANES), 1)
        high, low = split(spread_taps(taps, rows - DEC * cols + LEFT))
        main[:, :LANES] = high
        main[:, LANES:] = low
        row = lax.broadcasted_iota(jnp.int32, (EDGE, 2 * LANES), 0) % 4
        lane = lax.broadcasted_iota(jnp.int32, (EDGE, 2 * LANES), 1)
        lane = jnp.where(lane < LANES, lane, lane + width - 2 * LANES)
        sample = jnp.where(row < 2, row - 2, row + LANES - 2)
        high, low = split(spread_taps(taps, lane - DEC * sample + LEFT))
        edge[...] = jnp.concatenate([high.astype(FLOAT), low.astype(FLOAT)], axis=0).astype(HALF)

    for tile in range(out.shape[0]):
        block = raw[pl.ds(tile * channels, channels), :]
        product = jnp.dot(block, main[...], preferred_element_type=FLOAT)
        out[tile, :channels, :] = (product[:, :LANES] + product[:, LANES:]).astype(HALF)
        ends = jnp.concatenate([block[:, :LANES], block[:, width - LANES :]], axis=1)
        partial = lax.dot_general(
            edge[...], ends, (((1,), (1,)), ((), ())), preferred_element_type=FLOAT
        )
        partial = partial[:EDGE] + partial[EDGE:]
        row = lax.broadcasted_iota(jnp.int32, (EDGE, LANES), 0)
        picked = jnp.where(row < 4, partial[:, :LANES], partial[:, LANES:])
        out[tile, channels:, :] = picked.astype(HALF)


def filter_blocks(raw, fir_taps, tiles):
    channels = raw.shape[0] // tiles
    width = raw.shape[1]
    step = 2
    return pl.pallas_call(
        functools.partial(filter_body, channels=channels),
        out_shape=jax.ShapeDtypeStruct((tiles, channels + EDGE, LANES), HALF),
        grid=(tiles // step,),
        in_specs=[
            pl.BlockSpec(memory_space=pltpu.SMEM),
            pl.BlockSpec((step * channels, width), lambda i: (i, 0)),
        ],
        out_specs=pl.BlockSpec((step, channels + EDGE, LANES), lambda i: (i, 0, 0)),
        scratch_shapes=[
            pltpu.VMEM((width, 2 * LANES), HALF),
            pltpu.VMEM((2 * EDGE, 2 * LANES), HALF),
        ],
        compiler_params=pltpu.CompilerParams(vmem_limit_bytes=60 << 20),
        name="filter",
    )(fir_taps, raw)


def filter_whole(channel_block, fir_taps):
    padded = jnp.pad(channel_block.astype(FLOAT), ((0, 0), (2 * DEC, 2 * DEC)))
    rows = padded.shape[0]
    phased = jnp.transpose(padded.reshape(rows, -1, DEC), (2, 0, 1))
    filtered = jnp.zeros((rows, NT), FLOAT)
    for tap in range(TAPS):
        first_at = 2 * DEC - LEFT + tap
        begin = first_at // DEC
        filtered = filtered + fir_taps[tap] * phased[first_at % DEC, :, begin : begin + NT]
    blocks = filtered.astype(HALF).reshape(rows, NT // LANES, LANES).transpose(1, 0, 2)
    return jnp.concatenate([blocks, jnp.zeros((NT // LANES, EDGE, LANES), HALF)], axis=1)


def whiten_body(dead, blocks, table, edge_table, window, counts, white, real, imag, total, ends):
    step = pl.program_id(0)
    group = blocks.shape[0]
    channels = white.shape[0]
    left = jnp.concatenate([blocks[i, :channels, :] for i in range(group)], axis=1)
    part = jnp.dot(left, table[...], preferred_element_type=FLOAT)
    for i in range(group):
        at = pl.multiple_of((step * group + i) * EDGE, EDGE)
        ends[pl.ds(at, EDGE), :] = blocks[i, channels:, :].astype(FLOAT)

    @pl.when(step == 0)
    def _():
        total[...] = part

    @pl.when(step > 0)
    def _():
        total[...] += part

    @pl.when(step == pl.num_programs(0) - 1)
    def _():
        turned = ends[...].T
        lane = lax.broadcasted_iota(jnp.int32, turned.shape, 1) % EDGE
        first = jnp.where(lane < 4, turned, 0.0)
        second = jnp.where(lane < 4, 0.0, turned)
        edges = jnp.concatenate([first, second], axis=0).astype(HALF)
        spectrum = total[...] + jnp.dot(edges, edge_table[...], preferred_element_type=FLOAT)
        channel = lax.broadcasted_iota(jnp.int32, spectrum.shape, 0)
        spectrum = jnp.where(channel < dead[0], 0.0, spectrum)
        re, im = spectrum[:, :NF], spectrum[:, NF:]
        high, low = split(re * re + im * im)
        summed = jnp.dot(high, window[...], preferred_element_type=FLOAT)
        summed += jnp.dot(low, window[...], preferred_element_type=FLOAT)
        factor = lax.rsqrt(summed / counts[...] + 1e-05)
        re, im = re * factor, im * factor
        real[...] = re
        imag[...] = im
        white[:, :NF] = re.astype(HALF)
        white[:, NF:] = im.astype(HALF)


def whiten(blocks, dead):
    count, height, _ = blocks.shape
    channels = height - EDGE
    group = 4
    window, counts = window_table()
    return pl.pallas_call(
        whiten_body,
        out_shape=(
            jax.ShapeDtypeStruct((channels, 2 * NF), HALF),
            jax.ShapeDtypeStruct((channels, NF), FLOAT),
            jax.ShapeDtypeStruct((channels, NF), FLOAT),
        ),
        grid=(count // group,),
        in_specs=[
            pl.BlockSpec(memory_space=pltpu.SMEM),
            pl.BlockSpec((group, height, LANES), lambda i: (i, 0, 0)),
            pl.BlockSpec((group * LANES, 2 * NF), lambda i: (i, 0)),
            pl.BlockSpec((count * EDGE, 2 * NF), lambda i: (0, 0)),
            pl.BlockSpec((NF, NF), lambda i: (0, 0)),
            pl.BlockSpec((1, NF), lambda i: (0, 0)),
        ],
        out_specs=(
            pl.BlockSpec((channels, 2 * NF), lambda i: (0, 0)),
            pl.BlockSpec((channels, NF), lambda i: (0, 0)),
            pl.BlockSpec((channels, NF), lambda i: (0, 0)),
        ),
        scratch_shapes=[
            pltpu.VMEM((channels, 2 * NF), FLOAT),
            pltpu.VMEM((count * EDGE, LANES), FLOAT),
        ],
        compiler_params=pltpu.CompilerParams(vmem_limit_bytes=24 << 20),
        name="whiten",
    )(
        dead,
        blocks,
        jnp.asarray(table_rows(np.arange(NT))),
        jnp.asarray(table_rows(edge_samples())),
        jnp.asarray(window),
        jnp.asarray(counts),
    )


def send(value, shift, keep=lambda source: True):
    count = lax.axis_size("row")
    pairs = [(s, s - shift(s)) for s in range(count) if keep(s) and 0 <= s - shift(s) < count]
    return lax.ppermute(value, "row", pairs)


def beside(value, keep=lambda source: True):
    return send(value, lambda s: s - (s ^ 1), keep)


def gather_first(white):
    one = beside(white, lambda s: s % 2 == 1)
    return one, send(white, lambda s: 4), send(white, lambda s: s - (s ^ 2))


def gather_second(four, across):
    two = send(across, lambda s: 4, lambda s: s & 2 == 2)
    six = send(four, lambda s: 2)
    return two, six, send(four, lambda s: 3, lambda s: s % 2 == 0)


WHOLE = pl.BlockSpec(memory_space=pltpu.VMEM)
SCALAR = pl.BlockSpec(memory_space=pltpu.SMEM)


def pair(left, columns, band, offset):
    product = lax.dot_general(
        left, columns, (((1,), (1,)), ((), ())), preferred_element_type=FLOAT
    )
    scale = jnp.where(offset < band[0], 1.0 / math.sqrt(NF), 0.0)
    return (product * scale).astype(HALF)


def by_parity(even, odd):
    return jnp.where(lax.axis_index("row") % 2 == 0, even, odd)


def cost(channels, tiles):
    return pl.CostEstimate(
        flops=2 * LAGS * tiles * channels * channels * 2 * NF,
        bytes_accessed=2 * LAGS * channels * (2 * NF + tiles * channels),
        transcendentals=0,
    )


def own_body(band, real, imag, cosine, sine, white, lagged, out):
    c, s = cosine[0], sine[0]
    re, im = real[...], imag[...]
    lagged[0, :, :NF] = (re * c - im * s).astype(HALF)
    lagged[0, :, NF:] = (re * s + im * c).astype(HALF)
    out[0] = pair(lagged[0], white[...], band, 0)


def correlate_own(band, real, imag, white):
    channels = real.shape[0]
    cosine, sine = lag_tables()
    return pl.pallas_call(
        own_body,
        out_shape=(
            jax.ShapeDtypeStruct((LAGS, channels, 2 * NF), HALF),
            jax.ShapeDtypeStruct((LAGS, channels, channels), HALF),
        ),
        grid=(LAGS,),
        in_specs=[
            SCALAR,
            WHOLE,
            WHOLE,
            pl.BlockSpec((1, 1, NF), lambda i: (i, 0, 0)),
            pl.BlockSpec((1, 1, NF), lambda i: (i, 0, 0)),
            WHOLE,
        ],
        out_specs=(
            pl.BlockSpec((1, channels, 2 * NF), lambda i: (i, 0, 0)),
            pl.BlockSpec((1, channels, channels), lambda i: (i, 0, 0)),
        ),
        compiler_params=pltpu.CompilerParams(vmem_limit_bytes=16 << 20),
        cost_estimate=cost(channels, 1),
        name="correlate_own",
    )(band, real, imag, jnp.asarray(cosine[:, None]), jnp.asarray(sine[:, None]), white)


def near_body(band, lagged, one, four, four_beside, out):
    left = lagged[pl.program_id(0)]
    out[0, 0] = pair(left, four[...], band, 4)
    out[1, 0] = pair(left, four_beside[...], band, by_parity(5, 3))
    out[2, 0] = pair(left, one[...], band, 1)


def correlate_near(band, lagged, one, four, four_beside):
    channels = lagged.shape[1]
    return pl.pallas_call(
        near_body,
        out_shape=jax.ShapeDtypeStruct((3, LAGS, channels, channels), HALF),
        grid=(LAGS,),
        in_specs=[SCALAR, WHOLE, WHOLE, WHOLE, WHOLE],
        out_specs=pl.BlockSpec((3, 1, channels, channels), lambda i: (0, i, 0, 0)),
        compiler_params=pltpu.CompilerParams(vmem_limit_bytes=16 << 20),
        cost_estimate=cost(channels, 3),
        name="correlate_near",
    )(band, lagged, one, four, four_beside)


EVEN = (0, 3, 7, 8, 1, 2, 4, 5)
ODD = (0, 8, 7, 2, 1, 5, 4, 6)


def far_body(
    band, lagged, own, near, six, six_beside, seven, two, two_beside, across, across_beside,
    out, columns, sems, *, rows,
):
    step = pl.program_id(0)
    channels = six.shape[0]
    near_side = lax.axis_index("row") & 2 == 0

    @pl.when(step == 0)
    def _():
        for slot, (here, there) in enumerate(((across, two), (across_beside, two_beside))):

            @pl.when(near_side)
            def _():
                pltpu.make_async_copy(here, columns.at[slot], sems.at[slot]).start()

            @pl.when(jnp.logical_not(near_side))
            def _():
                pltpu.make_async_copy(there, columns.at[slot], sems.at[slot]).start()

        for slot in range(2):
            pltpu.make_async_copy(two, columns.at[slot], sems.at[slot]).wait()

    at = pl.ds(pl.multiple_of(step * rows, rows), rows)
    left = lagged[:, at, :].reshape(LAGS * rows, 2 * NF)
    far = [
        pair(left, tile, band, offset).reshape(LAGS, rows, channels)
        for tile, offset in (
            (six[...], 6),
            (six_beside[...], by_parity(7, 5)),
            (seven[...], 7),
            (columns[0], 2),
            (columns[1], by_parity(3, 1)),
        )
    ]
    even_row = lax.axis_index("row") % 2 == 0
    for lag in range(LAGS):
        for half in range(channels // LANES):
            lanes = slice(half * LANES, (half + 1) * LANES)
            planes = [own[lag, at, lanes]]
            planes += [near[index, lag, at, lanes] for index in range(3)]
            planes += [plane[lag, :, lanes] for plane in far]
            ordered = [
                planes[even] if even == odd else jnp.where(even_row, planes[even], planes[odd])
                for even, odd in zip(EVEN, ODD)
            ]
            out[:, lag, :, lanes] = pltpu.einshape("kab->akb", jnp.stack(ordered))


def correlate_far(band, lagged, own, near, *tiles):
    channels = lagged.shape[1]
    rows = 32
    return pl.pallas_call(
        functools.partial(far_body, rows=rows),
        out_shape=jax.ShapeDtypeStruct((channels, LAGS, NB, channels), HALF),
        grid=(channels // rows,),
        in_specs=[SCALAR] + [WHOLE] * 3 + [WHOLE] * 3 + [pl.BlockSpec(memory_space=pl.ANY)] * 4,
        out_specs=pl.BlockSpec((rows, LAGS, NB, channels), lambda i: (i, 0, 0, 0)),
        scratch_shapes=[
            pltpu.VMEM((2, channels, 2 * NF), HALF),
            pltpu.SemaphoreType.DMA((2,)),
        ],
        compiler_params=pltpu.CompilerParams(vmem_limit_bytes=24 << 20),
        cost_estimate=cost(channels, 5),
        name="correlate_far",
    )(band, lagged, own, near, *tiles)


def shards(raw, fir_taps, band_width, dead_count):
    tiles = lax.axis_size("row")
    if raw.shape[1] == DEC * LANES:
        blocks = filter_blocks(raw, fir_taps, tiles)
        blocks = lax.all_to_all(blocks, "row", split_axis=0, concat_axis=0, tiled=True)
    else:
        channel_block = lax.all_to_all(raw, "row", split_axis=0, concat_axis=1, tiled=True)
        blocks = filter_whole(channel_block, fir_taps)
    white, real, imag = whiten(blocks, dead_count)
    one, four, across = gather_first(white)
    lagged, own = correlate_own(band_width, real, imag, white)
    four, across, lagged = lax.optimization_barrier((four, across, lagged))
    two, six, seven = gather_second(four, across)
    across_beside = beside(across, lambda s: s & 2 == 0)
    near = correlate_near(band_width, lagged, one, four, beside(four))
    two, six, seven, near = lax.optimization_barrier((two, six, seven, near))
    two_beside = beside(two, lambda s: s & 2 == 2)
    return correlate_far(
        band_width, lagged, own, near, six, beside(six), seven, two, two_beside, across, across_beside
    )


def solution(mesh):
    return jax.shard_map(
        shards,
        mesh=mesh,
        in_specs=(P(None, ("win", "row")), P(), P("row"), P("row")),
        out_specs=P(("win", "row"), None, None, None),
        check_vma=False,
    )
```

```python
import functools
import math

import jax
import jax.numpy as jnp
import ml_dtypes
import numpy as np
from jax import lax
from jax.experimental import pallas as pl
from jax.experimental.pallas import tpu as pltpu
from jax.sharding import PartitionSpec as P

NT = 2048
NF = 512
DEC = 4
TAPS = 16
SMOOTH = 64
LAGS = 8
NB = 8
LEFT = (TAPS - DEC) // 2
LANES = 128
EDGE = 8
FLOAT = jnp.float32
HALF = jnp.bfloat16


def table_rows(samples):
    bins = np.arange(NF, dtype=np.int64)[None, :] + 1
    samples = np.asarray(samples, dtype=np.int64)[:, None]
    phases = (samples * bins % NT).astype(np.float64) * (2.0 * math.pi / NT)
    rows = np.concatenate([np.cos(phases), -np.sin(phases)], axis=1)
    inside = (samples >= 0) & (samples < NT)
    return np.where(inside, rows, 0.0).astype(ml_dtypes.bfloat16)


def edge_samples():
    blocks = NT // LANES
    offsets = np.array([-2, -1, LANES, LANES + 1] * 2)
    return (np.arange(blocks)[:, None] * LANES + offsets[None, :]).reshape(-1)


def window_table():
    ids = np.arange(NF)
    window = np.abs(ids[:, None] - ids[None, :]) <= SMOOTH
    counts = window.sum(axis=0).astype(np.float32)[None, :]
    return window.astype(ml_dtypes.bfloat16), counts


def lag_tables():
    lags = np.arange(LAGS, dtype=np.int64) - LAGS // 2
    bins = np.arange(NF, dtype=np.int64) + 1
    phases = ((lags % NT)[:, None] * bins[None, :] % NT) * (2.0 * math.pi / NT)
    return np.cos(phases).astype(np.float32), np.sin(phases).astype(np.float32)


def split(value):
    high = value.astype(HALF)
    low = (value - high.astype(FLOAT)).astype(HALF)
    return high, low


def spread_taps(taps, index):
    spread = jnp.zeros(index.shape, FLOAT)
    for tap in range(TAPS):
        spread = jnp.where(index == tap, taps[tap], spread)
    return spread


def filter_body(taps, raw, other, own, held, main, edge, sems, *, channels):
    width = raw.shape[1]
    step = pl.program_id(0)
    group = own.shape[0]
    count = held.shape[0] // 2
    chip = lax.axis_index("row") // 2
    parity = lax.axis_index("row") % 2

    @pl.when(step == 0)
    def _():
        for slot in range(2 * count):
            tile = (chip ^ (slot % count)) * 2 + (parity ^ (1 - slot // count))
            at = pl.ds(pl.multiple_of(tile * channels, channels), channels)
            pltpu.make_async_copy(raw.at[at], held.at[slot], sems.at[slot]).start()
        rows = lax.broadcasted_iota(jnp.int32, (width, LANES), 0)
        cols = lax.broadcasted_iota(jnp.int32, (width, LANES), 1)
        high, low = split(spread_taps(taps, rows - DEC * cols + LEFT))
        main[:, :LANES] = high
        main[:, LANES:] = low
        row = lax.broadcasted_iota(jnp.int32, (EDGE, 2 * LANES), 0) % 4
        lane = lax.broadcasted_iota(jnp.int32, (EDGE, 2 * LANES), 1)
        lane = jnp.where(lane < LANES, lane, lane + width - 2 * LANES)
        sample = jnp.where(row < 2, row - 2, row + LANES - 2)
        high, low = split(spread_taps(taps, lane - DEC * sample + LEFT))
        edge[...] = jnp.concatenate([high.astype(FLOAT), low.astype(FLOAT)], axis=0).astype(HALF)

    def run(out):
        slots = [step * group + index for index in range(group)]
        for slot in slots:
            pltpu.make_async_copy(raw.at[pl.ds(0, channels)], held.at[slot], sems.at[slot]).wait()
        for index, slot in enumerate(slots):
            block = held[slot]
            product = jnp.dot(block, main[...], preferred_element_type=FLOAT)
            out[index, :channels, :] = (product[:, :LANES] + product[:, LANES:]).astype(HALF)
            ends = jnp.concatenate([block[:, :LANES], block[:, width - LANES :]], axis=1)
            partial = lax.dot_general(
                edge[...], ends, (((1,), (1,)), ((), ())), preferred_element_type=FLOAT
            )
            partial = partial[:EDGE] + partial[EDGE:]
            row = lax.broadcasted_iota(jnp.int32, (EDGE, LANES), 0)
            picked = jnp.where(row < 4, partial[:, :LANES], partial[:, LANES:])
            out[index, channels:, :] = picked.astype(HALF)

    half = pl.num_programs(0) // 2
    pl.when(step < half)(lambda: run(other))
    pl.when(step >= half)(lambda: run(own))


def filter_blocks(raw, fir_taps, tiles):
    channels = raw.shape[0] // tiles
    width = raw.shape[1]
    chips = tiles // 2
    group = 4
    half = chips // group
    block = (group, channels + EDGE, LANES)
    return pl.pallas_call(
        functools.partial(filter_body, channels=channels),
        out_shape=(jax.ShapeDtypeStruct((chips, channels + EDGE, LANES), HALF),) * 2,
        grid=(2 * half,),
        in_specs=[
            pl.BlockSpec(memory_space=pltpu.SMEM),
            pl.BlockSpec(memory_space=pl.ANY),
        ],
        out_specs=(
            pl.BlockSpec(block, lambda i: (jnp.minimum(i, half - 1), 0, 0)),
            pl.BlockSpec(block, lambda i: (jnp.maximum(i - half, 0), 0, 0)),
        ),
        scratch_shapes=[
            pltpu.VMEM((tiles, channels, width), HALF),
            pltpu.VMEM((width, 2 * LANES), HALF),
            pltpu.VMEM((2 * EDGE, 2 * LANES), HALF),
            pltpu.SemaphoreType.DMA((tiles,)),
        ],
        compiler_params=pltpu.CompilerParams(vmem_limit_bytes=58 << 20),
        name="filter",
    )(fir_taps, raw)


def transpose_blocks(raw, fir_taps, tiles):
    other, own = filter_blocks(raw, fir_taps, tiles)
    came = lax.ppermute(other, "row", [(s, s ^ 1) for s in range(tiles)])
    pieces = [jnp.concatenate([own[d], came[d]], axis=0) for d in range(tiles // 2)]
    pieces = lax.optimization_barrier(pieces)
    return pieces[:1] + [
        lax.ppermute(pieces[d], "row", [(s, s ^ (2 * d)) for s in range(tiles)])
        for d in range(1, tiles // 2)
    ]


def filter_whole(channel_block, fir_taps):
    padded = jnp.pad(channel_block.astype(FLOAT), ((0, 0), (2 * DEC, 2 * DEC)))
    rows = padded.shape[0]
    phased = jnp.transpose(padded.reshape(rows, -1, DEC), (2, 0, 1))
    filtered = jnp.zeros((rows, NT), FLOAT)
    for tap in range(TAPS):
        first_at = 2 * DEC - LEFT + tap
        begin = first_at // DEC
        filtered = filtered + fir_taps[tap] * phased[first_at % DEC, :, begin : begin + NT]
    blocks = filtered.astype(HALF).reshape(rows, NT // LANES, LANES).transpose(1, 0, 2)
    blocks = jnp.concatenate([blocks, jnp.zeros((NT // LANES, EDGE, LANES), HALF)], axis=1)
    return [blocks[d : d + 2].reshape(-1, LANES) for d in range(0, NT // LANES, 2)]


def whiten_body(dead, table, edge_table, window, counts, *rest, count, ordered):
    pieces, white, real, imag, ends = rest[:count], *rest[count:]
    channels = white.shape[0]
    height = channels + EDGE
    chip = 0 if ordered else lax.axis_index("row") // 2
    parity = 0 if ordered else lax.axis_index("row") % 2

    spectrum = jnp.zeros((channels, 2 * NF), FLOAT)
    for index, piece in enumerate(pieces):
        source = index if ordered else chip ^ index
        mine, other = piece[:channels, :], piece[height : height + channels, :]
        if ordered:
            left = jnp.concatenate([mine, other], axis=1)
        else:
            left = jnp.concatenate(
                [jnp.where(parity == 0, mine, other), jnp.where(parity == 0, other, mine)], axis=1
            )
        for part in range(2):
            block = source * 2 + (part if ordered else part ^ parity)
            at = pl.ds(pl.multiple_of(block * EDGE, EDGE), EDGE)
            ends[at, :] = piece[part * height + channels : (part + 1) * height, :].astype(FLOAT)
        at = pl.ds(pl.multiple_of(source * (2 * LANES), 2 * LANES), 2 * LANES)
        spectrum += jnp.dot(left, table[at, :], preferred_element_type=FLOAT)

    turned = ends[...].T
    lane = lax.broadcasted_iota(jnp.int32, turned.shape, 1) % EDGE
    first = jnp.where(lane < 4, turned, 0.0)
    second = jnp.where(lane < 4, 0.0, turned)
    edges = jnp.concatenate([first, second], axis=0).astype(HALF)
    spectrum += jnp.dot(edges, edge_table[...], preferred_element_type=FLOAT)
    channel = lax.broadcasted_iota(jnp.int32, spectrum.shape, 0)
    spectrum = jnp.where(channel < dead[0], 0.0, spectrum)
    re, im = spectrum[:, :NF], spectrum[:, NF:]
    high, low = split(re * re + im * im)
    summed = jnp.dot(high, window[...], preferred_element_type=FLOAT)
    summed += jnp.dot(low, window[...], preferred_element_type=FLOAT)
    factor = lax.rsqrt(summed / counts[...] + 1e-05)
    re, im = re * factor, im * factor
    real[...] = re
    imag[...] = im
    white[:, :NF] = re.astype(HALF)
    white[:, NF:] = im.astype(HALF)


def whiten(pieces, dead, ordered):
    channels = pieces[0].shape[0] // 2 - EDGE
    blocks = 2 * len(pieces)
    window, counts = window_table()
    return pl.pallas_call(
        functools.partial(whiten_body, count=len(pieces), ordered=ordered),
        out_shape=(
            jax.ShapeDtypeStruct((channels, 2 * NF), HALF),
            jax.ShapeDtypeStruct((channels, NF), FLOAT),
            jax.ShapeDtypeStruct((channels, NF), FLOAT),
        ),
        in_specs=[pl.BlockSpec(memory_space=pltpu.SMEM)]
        + [pl.BlockSpec(memory_space=pltpu.VMEM)] * (4 + len(pieces)),
        out_specs=(pl.BlockSpec(memory_space=pltpu.VMEM),) * 3,
        scratch_shapes=[pltpu.VMEM((blocks * EDGE, LANES), FLOAT)],
        compiler_params=pltpu.CompilerParams(vmem_limit_bytes=24 << 20),
        name="whiten",
    )(
        dead,
        jnp.asarray(table_rows(np.arange(NT))),
        jnp.asarray(table_rows(edge_samples())),
        jnp.asarray(window),
        jnp.asarray(counts),
        *pieces,
    )


def send(value, shift, keep=lambda source: True):
    count = lax.axis_size("row")
    pairs = [(s, s - shift(s)) for s in range(count) if keep(s) and 0 <= s - shift(s) < count]
    return lax.ppermute(value, "row", pairs)


def beside(value, keep=lambda source: True):
    return send(value, lambda s: s - (s ^ 1), keep)


def gather_first(white):
    four = send(white, lambda s: 4)
    across = send(white, lambda s: s - (s ^ 2))
    return beside(white, lambda s: s % 2 == 1), four, across


def gather_second(four, across):
    six = send(four, lambda s: 2)
    two = send(across, lambda s: 4, lambda s: s & 2 == 2)
    return two, six, send(four, lambda s: 3, lambda s: s % 2 == 0)


WHOLE = pl.BlockSpec(memory_space=pltpu.VMEM)
SCALAR = pl.BlockSpec(memory_space=pltpu.SMEM)


def pair(left, columns, band, offset):
    product = lax.dot_general(
        left, columns, (((1,), (1,)), ((), ())), preferred_element_type=FLOAT
    )
    scale = jnp.where(offset < band[0], 1.0 / math.sqrt(NF), 0.0)
    return (product * scale).astype(HALF)


def by_parity(even, odd):
    return jnp.where(lax.axis_index("row") % 2 == 0, even, odd)


def cost(channels, tiles):
    return pl.CostEstimate(
        flops=2 * LAGS * tiles * channels * channels * 2 * NF,
        bytes_accessed=2 * LAGS * channels * (2 * NF + tiles * channels),
        transcendentals=0,
    )


def own_body(band, real, imag, cosine, sine, white, lagged, out):
    c, s = cosine[0], sine[0]
    re, im = real[...], imag[...]
    lagged[0, :, :NF] = (re * c - im * s).astype(HALF)
    lagged[0, :, NF:] = (re * s + im * c).astype(HALF)
    out[0] = pair(lagged[0], white[...], band, 0)


def correlate_own(band, real, imag, white):
    channels = real.shape[0]
    cosine, sine = lag_tables()
    return pl.pallas_call(
        own_body,
        out_shape=(
            jax.ShapeDtypeStruct((LAGS, channels, 2 * NF), HALF),
            jax.ShapeDtypeStruct((LAGS, channels, channels), HALF),
        ),
        grid=(LAGS,),
        in_specs=[
            SCALAR,
            WHOLE,
            WHOLE,
            pl.BlockSpec((1, 1, NF), lambda i: (i, 0, 0)),
            pl.BlockSpec((1, 1, NF), lambda i: (i, 0, 0)),
            WHOLE,
        ],
        out_specs=(
            pl.BlockSpec((1, channels, 2 * NF), lambda i: (i, 0, 0)),
            pl.BlockSpec((1, channels, channels), lambda i: (i, 0, 0)),
        ),
        compiler_params=pltpu.CompilerParams(vmem_limit_bytes=16 << 20),
        cost_estimate=cost(channels, 1),
        name="correlate_own",
    )(band, real, imag, jnp.asarray(cosine[:, None]), jnp.asarray(sine[:, None]), white)


def near_body(band, lagged, one, four, four_beside, out):
    left = lagged[pl.program_id(0)]
    out[0, 0] = pair(left, four[...], band, 4)
    out[1, 0] = pair(left, four_beside[...], band, by_parity(5, 3))
    out[2, 0] = pair(left, one[...], band, 1)


def correlate_near(band, lagged, one, four, four_beside):
    channels = lagged.shape[1]
    return pl.pallas_call(
        near_body,
        out_shape=jax.ShapeDtypeStruct((3, LAGS, channels, channels), HALF),
        grid=(LAGS,),
        in_specs=[SCALAR, WHOLE, WHOLE, WHOLE, WHOLE],
        out_specs=pl.BlockSpec((3, 1, channels, channels), lambda i: (0, i, 0, 0)),
        compiler_params=pltpu.CompilerParams(vmem_limit_bytes=16 << 20),
        cost_estimate=cost(channels, 3),
        name="correlate_near",
    )(band, lagged, one, four, four_beside)


EVEN = (0, 3, 7, 8, 1, 2, 4, 5)
ODD = (0, 8, 7, 2, 1, 5, 4, 6)


def far_body(
    band, lagged, own, near, six, six_beside, seven, two, two_beside, across, across_beside,
    out, columns, sems, *, rows,
):
    step = pl.program_id(0)
    channels = six.shape[0]
    near_side = lax.axis_index("row") & 2 == 0

    @pl.when(step == 0)
    def _():
        for slot, (here, there) in enumerate(((across, two), (across_beside, two_beside))):

            @pl.when(near_side)
            def _():
                pltpu.make_async_copy(here, columns.at[slot], sems.at[slot]).start()

            @pl.when(jnp.logical_not(near_side))
            def _():
                pltpu.make_async_copy(there, columns.at[slot], sems.at[slot]).start()

        for slot in range(2):
            pltpu.make_async_copy(two, columns.at[slot], sems.at[slot]).wait()

    at = pl.ds(pl.multiple_of(step * rows, rows), rows)
    left = lagged[:, at, :].reshape(LAGS * rows, 2 * NF)
    far = [
        pair(left, tile, band, offset).reshape(LAGS, rows, channels)
        for tile, offset in (
            (six[...], 6),
            (six_beside[...], by_parity(7, 5)),
            (seven[...], 7),
            (columns[0], 2),
            (columns[1], by_parity(3, 1)),
        )
    ]
    even_row = lax.axis_index("row") % 2 == 0
    for lag in range(LAGS):
        for half in range(channels // LANES):
            lanes = slice(half * LANES, (half + 1) * LANES)
            planes = [own[lag, at, lanes]]
            planes += [near[index, lag, at, lanes] for index in range(3)]
            planes += [plane[lag, :, lanes] for plane in far]
            ordered = [
                planes[even] if even == odd else jnp.where(even_row, planes[even], planes[odd])
                for even, odd in zip(EVEN, ODD)
            ]
            out[:, lag, :, lanes] = pltpu.einshape("kab->akb", jnp.stack(ordered))


def correlate_far(band, lagged, own, near, *tiles):
    channels = lagged.shape[1]
    rows = 32
    return pl.pallas_call(
        functools.partial(far_body, rows=rows),
        out_shape=jax.ShapeDtypeStruct((channels, LAGS, NB, channels), HALF),
        grid=(channels // rows,),
        in_specs=[SCALAR] + [WHOLE] * 3 + [WHOLE] * 3 + [pl.BlockSpec(memory_space=pl.ANY)] * 4,
        out_specs=pl.BlockSpec((rows, LAGS, NB, channels), lambda i: (i, 0, 0, 0)),
        scratch_shapes=[
            pltpu.VMEM((2, channels, 2 * NF), HALF),
            pltpu.SemaphoreType.DMA((2,)),
        ],
        compiler_params=pltpu.CompilerParams(vmem_limit_bytes=24 << 20),
        cost_estimate=cost(channels, 5),
        name="correlate_far",
    )(band, lagged, own, near, *tiles)


def shards(raw, fir_taps, band_width, dead_count):
    tiles = lax.axis_size("row")
    if raw.shape[1] == DEC * LANES:
        white, real, imag = whiten(transpose_blocks(raw, fir_taps, tiles), dead_count, False)
    else:
        channel_block = lax.all_to_all(raw, "row", split_axis=0, concat_axis=1, tiled=True)
        white, real, imag = whiten(filter_whole(channel_block, fir_taps), dead_count, True)
    one, four, across = gather_first(white)
    lagged, own = correlate_own(band_width, real, imag, white)
    four, across, lagged = lax.optimization_barrier((four, across, lagged))
    two, six, seven = gather_second(four, across)
    across_beside = beside(across, lambda s: s & 2 == 0)
    near = correlate_near(band_width, lagged, one, four, beside(four))
    two, six, seven, near = lax.optimization_barrier((two, six, seven, near))
    two_beside = beside(two, lambda s: s & 2 == 2)
    return correlate_far(
        band_width, lagged, own, near, six, beside(six), seven, two, two_beside, across, across_beside
    )


def solution(mesh):
    return jax.shard_map(
        shards,
        mesh=mesh,
        in_specs=(P(None, ("win", "row")), P(), P("row"), P("row")),
        out_specs=P(("win", "row"), None, None, None),
        check_vma=False,
    )
```

```python
import functools
import math

import jax
import jax.numpy as jnp
import ml_dtypes
import numpy as np
from jax import lax
from jax.experimental import pallas as pl
from jax.experimental.pallas import tpu as pltpu
from jax.sharding import PartitionSpec as P

NT = 2048
NF = 512
DEC = 4
TAPS = 16
SMOOTH = 64
LAGS = 8
NB = 8
LEFT = (TAPS - DEC) // 2
LANES = 128
EDGE = 8
FLOAT = jnp.float32
HALF = jnp.bfloat16


def table_rows(samples):
    bins = np.arange(NF, dtype=np.int64)[None, :] + 1
    samples = np.asarray(samples, dtype=np.int64)[:, None]
    phases = (samples * bins % NT).astype(np.float64) * (2.0 * math.pi / NT)
    rows = np.concatenate([np.cos(phases), -np.sin(phases)], axis=1)
    inside = (samples >= 0) & (samples < NT)
    return np.where(inside, rows, 0.0).astype(ml_dtypes.bfloat16)


def edge_samples():
    blocks = NT // LANES
    offsets = np.array([-2, -1, LANES, LANES + 1] * 2)
    return (np.arange(blocks)[:, None] * LANES + offsets[None, :]).reshape(-1)


def window_table():
    ids = np.arange(NF)
    window = np.abs(ids[:, None] - ids[None, :]) <= SMOOTH
    counts = window.sum(axis=0).astype(np.float32)[None, :]
    return window.astype(ml_dtypes.bfloat16), counts


def lag_tables():
    lags = np.arange(LAGS, dtype=np.int64) - LAGS // 2
    bins = np.arange(NF, dtype=np.int64) + 1
    phases = ((lags % NT)[:, None] * bins[None, :] % NT) * (2.0 * math.pi / NT)
    return np.cos(phases).astype(np.float32), np.sin(phases).astype(np.float32)


def split(value):
    high = value.astype(HALF)
    low = (value - high.astype(FLOAT)).astype(HALF)
    return high, low


def spread_taps(taps, index):
    spread = jnp.zeros(index.shape, FLOAT)
    for tap in range(TAPS):
        spread = jnp.where(index == tap, taps[tap], spread)
    return spread


def filter_body(taps, raw, other, own, held, main, edge, sems, *, channels):
    width = raw.shape[1]
    step = pl.program_id(0)
    group = own.shape[0]
    count = held.shape[0] // 2
    chip = lax.axis_index("row") // 2
    parity = lax.axis_index("row") % 2

    @pl.when(step == 0)
    def _():
        for slot in range(2 * count):
            tile = (chip ^ (slot % count)) * 2 + (parity ^ (1 - slot // count))
            at = pl.ds(pl.multiple_of(tile * channels, channels), channels)
            pltpu.make_async_copy(raw.at[at], held.at[slot], sems.at[slot]).start()
        rows = lax.broadcasted_iota(jnp.int32, (width, LANES), 0)
        cols = lax.broadcasted_iota(jnp.int32, (width, LANES), 1)
        high, low = split(spread_taps(taps, rows - DEC * cols + LEFT))
        main[:, :LANES] = high
        main[:, LANES:] = low
        row = lax.broadcasted_iota(jnp.int32, (EDGE, 2 * LANES), 0) % 4
        lane = lax.broadcasted_iota(jnp.int32, (EDGE, 2 * LANES), 1)
        lane = jnp.where(lane < LANES, lane, lane + width - 2 * LANES)
        sample = jnp.where(row < 2, row - 2, row + LANES - 2)
        high, low = split(spread_taps(taps, lane - DEC * sample + LEFT))
        edge[...] = jnp.concatenate([high.astype(FLOAT), low.astype(FLOAT)], axis=0).astype(HALF)

    def run(out):
        slots = [step * group + index for index in range(group)]
        for slot in slots:
            pltpu.make_async_copy(raw.at[pl.ds(0, channels)], held.at[slot], sems.at[slot]).wait()
        for index, slot in enumerate(slots):
            block = held[slot]
            product = jnp.dot(block, main[...], preferred_element_type=FLOAT)
            out[index, :channels, :] = (product[:, :LANES] + product[:, LANES:]).astype(HALF)
            ends = jnp.concatenate([block[:, :LANES], block[:, width - LANES :]], axis=1)
            partial = lax.dot_general(
                edge[...], ends, (((1,), (1,)), ((), ())), preferred_element_type=FLOAT
            )
            partial = partial[:EDGE] + partial[EDGE:]
            row = lax.broadcasted_iota(jnp.int32, (EDGE, LANES), 0)
            picked = jnp.where(row < 4, partial[:, :LANES], partial[:, LANES:])
            out[index, channels:, :] = picked.astype(HALF)

    half = pl.num_programs(0) // 2
    pl.when(step < half)(lambda: run(other))
    pl.when(step >= half)(lambda: run(own))


def filter_blocks(raw, fir_taps, tiles):
    channels = raw.shape[0] // tiles
    width = raw.shape[1]
    chips = tiles // 2
    group = 4
    half = chips // group
    block = (group, channels + EDGE, LANES)
    return pl.pallas_call(
        functools.partial(filter_body, channels=channels),
        out_shape=(jax.ShapeDtypeStruct((chips, channels + EDGE, LANES), HALF),) * 2,
        grid=(2 * half,),
        in_specs=[
            pl.BlockSpec(memory_space=pltpu.SMEM),
            pl.BlockSpec(memory_space=pl.ANY),
        ],
        out_specs=(
            pl.BlockSpec(block, lambda i: (jnp.minimum(i, half - 1), 0, 0)),
            pl.BlockSpec(block, lambda i: (jnp.maximum(i - half, 0), 0, 0)),
        ),
        scratch_shapes=[
            pltpu.VMEM((tiles, channels, width), HALF),
            pltpu.VMEM((width, 2 * LANES), HALF),
            pltpu.VMEM((2 * EDGE, 2 * LANES), HALF),
            pltpu.SemaphoreType.DMA((tiles,)),
        ],
        compiler_params=pltpu.CompilerParams(vmem_limit_bytes=58 << 20),
        name="filter",
    )(fir_taps, raw)


def transpose_blocks(raw, fir_taps, tiles):
    other, own = filter_blocks(raw, fir_taps, tiles)
    came = lax.ppermute(other, "row", [(s, s ^ 1) for s in range(tiles)])
    pieces = [jnp.concatenate([own[d], came[d]], axis=0) for d in range(tiles // 2)]
    pieces = lax.optimization_barrier(pieces)
    return pieces[:1] + [
        lax.ppermute(pieces[d], "row", [(s, s ^ (2 * d)) for s in range(tiles)])
        for d in range(1, tiles // 2)
    ]


def filter_whole(channel_block, fir_taps):
    padded = jnp.pad(channel_block.astype(FLOAT), ((0, 0), (2 * DEC, 2 * DEC)))
    rows = padded.shape[0]
    phased = jnp.transpose(padded.reshape(rows, -1, DEC), (2, 0, 1))
    filtered = jnp.zeros((rows, NT), FLOAT)
    for tap in range(TAPS):
        first_at = 2 * DEC - LEFT + tap
        begin = first_at // DEC
        filtered = filtered + fir_taps[tap] * phased[first_at % DEC, :, begin : begin + NT]
    blocks = filtered.astype(HALF).reshape(rows, NT // LANES, LANES).transpose(1, 0, 2)
    blocks = jnp.concatenate([blocks, jnp.zeros((NT // LANES, EDGE, LANES), HALF)], axis=1)
    return [blocks[d : d + 2].reshape(-1, LANES) for d in range(0, NT // LANES, 2)]


def whiten_body(dead, table, edge_table, window, counts, *rest, count, ordered):
    pieces, white, real, imag, ends = rest[:count], *rest[count:]
    channels = white.shape[0]
    height = channels + EDGE
    chip = 0 if ordered else lax.axis_index("row") // 2
    parity = 0 if ordered else lax.axis_index("row") % 2

    spectrum = jnp.zeros((channels, 2 * NF), FLOAT)
    for index, piece in enumerate(pieces):
        source = index if ordered else chip ^ index
        mine, other = piece[:channels, :], piece[height : height + channels, :]
        if ordered:
            left = jnp.concatenate([mine, other], axis=1)
        else:
            left = jnp.concatenate(
                [jnp.where(parity == 0, mine, other), jnp.where(parity == 0, other, mine)], axis=1
            )
        for part in range(2):
            block = source * 2 + (part if ordered else part ^ parity)
            at = pl.ds(pl.multiple_of(block * EDGE, EDGE), EDGE)
            ends[at, :] = piece[part * height + channels : (part + 1) * height, :].astype(FLOAT)
        at = pl.ds(pl.multiple_of(source * (2 * LANES), 2 * LANES), 2 * LANES)
        spectrum += jnp.dot(left, table[at, :], preferred_element_type=FLOAT)

    turned = ends[...].T
    lane = lax.broadcasted_iota(jnp.int32, turned.shape, 1) % EDGE
    first = jnp.where(lane < 4, turned, 0.0)
    second = jnp.where(lane < 4, 0.0, turned)
    edges = jnp.concatenate([first, second], axis=0).astype(HALF)
    spectrum += jnp.dot(edges, edge_table[...], preferred_element_type=FLOAT)
    channel = lax.broadcasted_iota(jnp.int32, spectrum.shape, 0)
    spectrum = jnp.where(channel < dead[0], 0.0, spectrum)
    re, im = spectrum[:, :NF], spectrum[:, NF:]
    high, low = split(re * re + im * im)
    summed = jnp.dot(high, window[...], preferred_element_type=FLOAT)
    summed += jnp.dot(low, window[...], preferred_element_type=FLOAT)
    factor = lax.rsqrt(summed / counts[...] + 1e-05)
    re, im = re * factor, im * factor
    real[...] = re
    imag[...] = im
    white[:, :NF] = re.astype(HALF)
    white[:, NF:] = im.astype(HALF)


def whiten(pieces, dead, ordered):
    channels = pieces[0].shape[0] // 2 - EDGE
    blocks = 2 * len(pieces)
    window, counts = window_table()
    return pl.pallas_call(
        functools.partial(whiten_body, count=len(pieces), ordered=ordered),
        out_shape=(
            jax.ShapeDtypeStruct((channels, 2 * NF), HALF),
            jax.ShapeDtypeStruct((channels, NF), FLOAT),
            jax.ShapeDtypeStruct((channels, NF), FLOAT),
        ),
        in_specs=[pl.BlockSpec(memory_space=pltpu.SMEM)]
        + [pl.BlockSpec(memory_space=pltpu.VMEM)] * (4 + len(pieces)),
        out_specs=(pl.BlockSpec(memory_space=pltpu.VMEM),) * 3,
        scratch_shapes=[pltpu.VMEM((blocks * EDGE, LANES), FLOAT)],
        compiler_params=pltpu.CompilerParams(vmem_limit_bytes=24 << 20),
        name="whiten",
    )(
        dead,
        jnp.asarray(table_rows(np.arange(NT))),
        jnp.asarray(table_rows(edge_samples())),
        jnp.asarray(window),
        jnp.asarray(counts),
        *pieces,
    )


def send(value, shift, keep=lambda source: True):
    count = lax.axis_size("row")
    pairs = [(s, s - shift(s)) for s in range(count) if keep(s) and 0 <= s - shift(s) < count]
    return lax.ppermute(value, "row", pairs)


def beside(value, keep=lambda source: True):
    return send(value, lambda s: s - (s ^ 1), keep)


def gather_first(white):
    four = send(white, lambda s: 4)
    across = send(white, lambda s: s - (s ^ 2))
    return beside(white, lambda s: s % 2 == 1), four, across


def gather_second(four, across):
    six = send(four, lambda s: 2)
    two = send(across, lambda s: 4, lambda s: s & 2 == 2)
    return two, six, send(four, lambda s: 3, lambda s: s % 2 == 0)


WHOLE = pl.BlockSpec(memory_space=pltpu.VMEM)
SCALAR = pl.BlockSpec(memory_space=pltpu.SMEM)


def pair(left, columns, band, offset):
    product = lax.dot_general(
        left, columns, (((1,), (1,)), ((), ())), preferred_element_type=FLOAT
    )
    scale = jnp.where(offset < band[0], 1.0 / math.sqrt(NF), 0.0)
    return (product * scale).astype(HALF)


def by_parity(even, odd):
    return jnp.where(lax.axis_index("row") % 2 == 0, even, odd)


def cost(channels, tiles):
    return pl.CostEstimate(
        flops=2 * LAGS * tiles * channels * channels * 2 * NF,
        bytes_accessed=2 * LAGS * channels * (2 * NF + tiles * channels),
        transcendentals=0,
    )


def own_body(band, real, imag, cosine, sine, white, lagged, out):
    c, s = cosine[0], sine[0]
    re, im = real[...], imag[...]
    lagged[0, :, :NF] = (re * c - im * s).astype(HALF)
    lagged[0, :, NF:] = (re * s + im * c).astype(HALF)
    out[0] = pair(lagged[0], white[...], band, 0)


def correlate_own(band, real, imag, white):
    channels = real.shape[0]
    cosine, sine = lag_tables()
    return pl.pallas_call(
        own_body,
        out_shape=(
            jax.ShapeDtypeStruct((LAGS, channels, 2 * NF), HALF),
            jax.ShapeDtypeStruct((LAGS, channels, channels), HALF),
        ),
        grid=(LAGS,),
        in_specs=[
            SCALAR,
            WHOLE,
            WHOLE,
            pl.BlockSpec((1, 1, NF), lambda i: (i, 0, 0)),
            pl.BlockSpec((1, 1, NF), lambda i: (i, 0, 0)),
            WHOLE,
        ],
        out_specs=(
            pl.BlockSpec((1, channels, 2 * NF), lambda i: (i, 0, 0)),
            pl.BlockSpec((1, channels, channels), lambda i: (i, 0, 0)),
        ),
        compiler_params=pltpu.CompilerParams(vmem_limit_bytes=16 << 20),
        cost_estimate=cost(channels, 1),
        name="correlate_own",
    )(band, real, imag, jnp.asarray(cosine[:, None]), jnp.asarray(sine[:, None]), white)


def near_body(band, lagged, one, four, four_beside, seven, two, across, out, columns, sem):
    first = pl.program_id(0) == 0
    near_side = lax.axis_index("row") & 2 == 0
    pl.when(first & near_side)(pltpu.make_async_copy(across, columns, sem).start)
    pl.when(first & jnp.logical_not(near_side))(pltpu.make_async_copy(two, columns, sem).start)
    pl.when(first)(pltpu.make_async_copy(two, columns, sem).wait)
    left = lagged[pl.program_id(0)]
    out[0, 0] = pair(left, four[...], band, 4)
    out[1, 0] = pair(left, four_beside[...], band, by_parity(5, 3))
    out[2, 0] = pair(left, one[...], band, 1)
    out[3, 0] = pair(left, seven[...], band, 7)
    out[4, 0] = pair(left, columns[...], band, 2)


def correlate_near(band, lagged, *tiles):
    channels = lagged.shape[1]
    return pl.pallas_call(
        near_body,
        out_shape=jax.ShapeDtypeStruct((5, LAGS, channels, channels), HALF),
        grid=(LAGS,),
        in_specs=[SCALAR] + [WHOLE] * 5 + [pl.BlockSpec(memory_space=pl.ANY)] * 2,
        out_specs=pl.BlockSpec((5, 1, channels, channels), lambda i: (0, i, 0, 0)),
        scratch_shapes=[pltpu.VMEM((channels, 2 * NF), HALF), pltpu.SemaphoreType.DMA],
        compiler_params=pltpu.CompilerParams(vmem_limit_bytes=16 << 20),
        cost_estimate=cost(channels, 5),
        name="correlate_near",
    )(band, lagged, *tiles)


EVEN = (0, 3, 5, 8, 1, 2, 6, 7)
ODD = (0, 8, 5, 2, 1, 7, 6, 4)


def far_body(
    band, lagged, own, near, six, six_beside, two_beside, across_beside, out, columns, sem,
    *, rows,
):
    step = pl.program_id(0)
    channels = six_beside.shape[0]
    first = step == 0
    near_side = lax.axis_index("row") & 2 == 0
    pl.when(first & near_side)(pltpu.make_async_copy(across_beside, columns, sem).start)
    pl.when(first & jnp.logical_not(near_side))(
        pltpu.make_async_copy(two_beside, columns, sem).start
    )
    pl.when(first)(pltpu.make_async_copy(two_beside, columns, sem).wait)

    def run(order, offsets):
        at = pl.ds(pl.multiple_of(step * rows, rows), rows)
        left = lagged[:, at, :].reshape(LAGS * rows, 2 * NF)
        far = [
            pair(left, tile, band, offset).reshape(LAGS, rows, channels)
            for tile, offset in zip((six[...], six_beside[...], columns[...]), offsets)
        ]
        for lag in range(LAGS):
            for half in range(channels // LANES):
                lanes = slice(half * LANES, (half + 1) * LANES)
                planes = []
                for plane in order:
                    if plane == 0:
                        planes.append(own[lag, at, lanes])
                    elif plane < 6:
                        planes.append(near[plane - 1, lag, at, lanes])
                    else:
                        planes.append(far[plane - 6][lag, :, lanes])
                out[:, lag, :, lanes] = pltpu.einshape("kab->akb", jnp.stack(planes))

    is_even = lax.axis_index("row") % 2 == 0
    pl.when(is_even)(lambda: run(EVEN, (6, 7, 3)))
    pl.when(jnp.logical_not(is_even))(lambda: run(ODD, (6, 5, 1)))


def correlate_far(band, lagged, own, near, *tiles):
    channels = lagged.shape[1]
    rows = 32
    return pl.pallas_call(
        functools.partial(far_body, rows=rows),
        out_shape=jax.ShapeDtypeStruct((channels, LAGS, NB, channels), HALF),
        grid=(channels // rows,),
        in_specs=[SCALAR] + [WHOLE] * 5 + [pl.BlockSpec(memory_space=pl.ANY)] * 2,
        out_specs=pl.BlockSpec((rows, LAGS, NB, channels), lambda i: (i, 0, 0, 0)),
        scratch_shapes=[pltpu.VMEM((channels, 2 * NF), HALF), pltpu.SemaphoreType.DMA],
        compiler_params=pltpu.CompilerParams(vmem_limit_bytes=24 << 20),
        cost_estimate=cost(channels, 3),
        name="correlate_far",
    )(band, lagged, own, near, *tiles)


def shards(raw, fir_taps, band_width, dead_count):
    tiles = lax.axis_size("row")
    if raw.shape[1] == DEC * LANES:
        white, real, imag = whiten(transpose_blocks(raw, fir_taps, tiles), dead_count, False)
    else:
        channel_block = lax.all_to_all(raw, "row", split_axis=0, concat_axis=1, tiled=True)
        white, real, imag = whiten(filter_whole(channel_block, fir_taps), dead_count, True)
    one, four, across = gather_first(white)
    lagged, own = correlate_own(band_width, real, imag, white)
    four, across, lagged = lax.optimization_barrier((four, across, lagged))
    two, six, seven = gather_second(four, across)
    across_beside = beside(across, lambda s: s & 2 == 0)
    four_beside = beside(four)
    near = correlate_near(band_width, lagged, one, four, four_beside, seven, two, across)
    two_beside = beside(two, lambda s: s & 2 == 2)
    six, near, two_beside = lax.optimization_barrier((six, near, two_beside))
    six_beside = beside(six)
    return correlate_far(band_width, lagged, own, near, six, six_beside, two_beside, across_beside)


def solution(mesh):
    return jax.shard_map(
        shards,
        mesh=mesh,
        in_specs=(P(None, ("win", "row")), P(), P("row"), P("row")),
        out_specs=P(("win", "row"), None, None, None),
        check_vma=False,
    )
```

```python
import functools
import math

import jax
import jax.numpy as jnp
import ml_dtypes
import numpy as np
from jax import lax
from jax.experimental import pallas as pl
from jax.experimental.pallas import tpu as pltpu
from jax.sharding import PartitionSpec as P

NT = 2048
NF = 512
DEC = 4
TAPS = 16
SMOOTH = 64
LAGS = 8
NB = 8
LEFT = (TAPS - DEC) // 2
LANES = 128
EDGE = 8
FLOAT = jnp.float32
HALF = jnp.bfloat16


def table_rows(samples):
    bins = np.arange(NF, dtype=np.int64)[None, :] + 1
    samples = np.asarray(samples, dtype=np.int64)[:, None]
    phases = (samples * bins % NT).astype(np.float64) * (2.0 * math.pi / NT)
    rows = np.concatenate([np.cos(phases), -np.sin(phases)], axis=1)
    inside = (samples >= 0) & (samples < NT)
    return np.where(inside, rows, 0.0).astype(ml_dtypes.bfloat16)


def edge_samples():
    blocks = NT // LANES
    offsets = np.array([-2, -1, LANES, LANES + 1] * 2)
    return (np.arange(blocks)[:, None] * LANES + offsets[None, :]).reshape(-1)


def window_table():
    ids = np.arange(NF)
    window = np.abs(ids[:, None] - ids[None, :]) <= SMOOTH
    counts = window.sum(axis=0).astype(np.float32)[None, :]
    return window.astype(ml_dtypes.bfloat16), counts


def lag_tables():
    lags = np.arange(LAGS, dtype=np.int64) - LAGS // 2
    bins = np.arange(NF, dtype=np.int64) + 1
    phases = ((lags % NT)[:, None] * bins[None, :] % NT) * (2.0 * math.pi / NT)
    return np.cos(phases).astype(np.float32), np.sin(phases).astype(np.float32)


def split(value):
    high = value.astype(HALF)
    low = (value - high.astype(FLOAT)).astype(HALF)
    return high, low


def spread_taps(taps, index):
    spread = jnp.zeros(index.shape, FLOAT)
    for tap in range(TAPS):
        spread = jnp.where(index == tap, taps[tap], spread)
    return spread


def filter_body(taps, raw, other, own, held, main, edge, sems, *, channels):
    width = raw.shape[1]
    step = pl.program_id(0)
    group = own.shape[0]
    count = held.shape[0] // 2
    chip = lax.axis_index("row") // 2
    parity = lax.axis_index("row") % 2

    @pl.when(step == 0)
    def _():
        for slot in range(2 * count):
            tile = (chip ^ (slot % count)) * 2 + (parity ^ (1 - slot // count))
            at = pl.ds(pl.multiple_of(tile * channels, channels), channels)
            pltpu.make_async_copy(raw.at[at], held.at[slot], sems.at[slot]).start()
        rows = lax.broadcasted_iota(jnp.int32, (width, LANES), 0)
        cols = lax.broadcasted_iota(jnp.int32, (width, LANES), 1)
        high, low = split(spread_taps(taps, rows - DEC * cols + LEFT))
        main[:, :LANES] = high
        main[:, LANES:] = low
        row = lax.broadcasted_iota(jnp.int32, (EDGE, 2 * LANES), 0) % 4
        lane = lax.broadcasted_iota(jnp.int32, (EDGE, 2 * LANES), 1)
        lane = jnp.where(lane < LANES, lane, lane + width - 2 * LANES)
        sample = jnp.where(row < 2, row - 2, row + LANES - 2)
        high, low = split(spread_taps(taps, lane - DEC * sample + LEFT))
        edge[...] = jnp.concatenate([high.astype(FLOAT), low.astype(FLOAT)], axis=0).astype(HALF)

    def run(out):
        slots = [step * group + index for index in range(group)]
        for slot in slots:
            pltpu.make_async_copy(raw.at[pl.ds(0, channels)], held.at[slot], sems.at[slot]).wait()
        for index, slot in enumerate(slots):
            block = held[slot]
            product = jnp.dot(block, main[...], preferred_element_type=FLOAT)
            out[index, :channels, :] = (product[:, :LANES] + product[:, LANES:]).astype(HALF)
            ends = jnp.concatenate([block[:, :LANES], block[:, width - LANES :]], axis=1)
            partial = lax.dot_general(
                edge[...], ends, (((1,), (1,)), ((), ())), preferred_element_type=FLOAT
            )
            partial = partial[:EDGE] + partial[EDGE:]
            row = lax.broadcasted_iota(jnp.int32, (EDGE, LANES), 0)
            picked = jnp.where(row < 4, partial[:, :LANES], partial[:, LANES:])
            out[index, channels:, :] = picked.astype(HALF)

    half = pl.num_programs(0) // 2
    pl.when(step < half)(lambda: run(other))
    pl.when(step >= half)(lambda: run(own))


def filter_blocks(raw, fir_taps, tiles):
    channels = raw.shape[0] // tiles
    width = raw.shape[1]
    chips = tiles // 2
    group = 4
    half = chips // group
    block = (group, channels + EDGE, LANES)
    return pl.pallas_call(
        functools.partial(filter_body, channels=channels),
        out_shape=(jax.ShapeDtypeStruct((chips, channels + EDGE, LANES), HALF),) * 2,
        grid=(2 * half,),
        in_specs=[
            pl.BlockSpec(memory_space=pltpu.SMEM),
            pl.BlockSpec(memory_space=pl.ANY),
        ],
        out_specs=(
            pl.BlockSpec(block, lambda i: (jnp.minimum(i, half - 1), 0, 0)),
            pl.BlockSpec(block, lambda i: (jnp.maximum(i - half, 0), 0, 0)),
        ),
        scratch_shapes=[
            pltpu.VMEM((tiles, channels, width), HALF),
            pltpu.VMEM((width, 2 * LANES), HALF),
            pltpu.VMEM((2 * EDGE, 2 * LANES), HALF),
            pltpu.SemaphoreType.DMA((tiles,)),
        ],
        compiler_params=pltpu.CompilerParams(vmem_limit_bytes=58 << 20),
        name="filter",
    )(fir_taps, raw)


def transpose_blocks(raw, fir_taps, tiles):
    other, own = filter_blocks(raw, fir_taps, tiles)
    came = lax.ppermute(other, "row", [(s, s ^ 1) for s in range(tiles)])
    pieces = [jnp.concatenate([own[d], came[d]], axis=0) for d in range(tiles // 2)]
    pieces = lax.optimization_barrier(pieces)
    return pieces[:1] + [
        lax.ppermute(pieces[d], "row", [(s, s ^ (2 * d)) for s in range(tiles)])
        for d in range(1, tiles // 2)
    ]


def filter_whole(channel_block, fir_taps):
    padded = jnp.pad(channel_block.astype(FLOAT), ((0, 0), (2 * DEC, 2 * DEC)))
    rows = padded.shape[0]
    phased = jnp.transpose(padded.reshape(rows, -1, DEC), (2, 0, 1))
    filtered = jnp.zeros((rows, NT), FLOAT)
    for tap in range(TAPS):
        first_at = 2 * DEC - LEFT + tap
        begin = first_at // DEC
        filtered = filtered + fir_taps[tap] * phased[first_at % DEC, :, begin : begin + NT]
    blocks = filtered.astype(HALF).reshape(rows, NT // LANES, LANES).transpose(1, 0, 2)
    blocks = jnp.concatenate([blocks, jnp.zeros((NT // LANES, EDGE, LANES), HALF)], axis=1)
    return [blocks[d : d + 2].reshape(-1, LANES) for d in range(0, NT // LANES, 2)]


def whiten_body(dead, table, edge_table, window, counts, *rest, count, ordered):
    pieces, white, real, imag, ends = rest[:count], *rest[count:]
    channels = white.shape[0]
    height = channels + EDGE
    chip = 0 if ordered else lax.axis_index("row") // 2
    parity = 0 if ordered else lax.axis_index("row") % 2

    spectrum = jnp.zeros((channels, 2 * NF), FLOAT)
    for index, piece in enumerate(pieces):
        source = index if ordered else chip ^ index
        mine, other = piece[:channels, :], piece[height : height + channels, :]
        if ordered:
            left = jnp.concatenate([mine, other], axis=1)
        else:
            left = jnp.concatenate(
                [jnp.where(parity == 0, mine, other), jnp.where(parity == 0, other, mine)], axis=1
            )
        for part in range(2):
            block = source * 2 + (part if ordered else part ^ parity)
            at = pl.ds(pl.multiple_of(block * EDGE, EDGE), EDGE)
            ends[at, :] = piece[part * height + channels : (part + 1) * height, :].astype(FLOAT)
        at = pl.ds(pl.multiple_of(source * (2 * LANES), 2 * LANES), 2 * LANES)
        spectrum += jnp.dot(left, table[at, :], preferred_element_type=FLOAT)

    turned = ends[...].T
    lane = lax.broadcasted_iota(jnp.int32, turned.shape, 1) % EDGE
    first = jnp.where(lane < 4, turned, 0.0)
    second = jnp.where(lane < 4, 0.0, turned)
    edges = jnp.concatenate([first, second], axis=0).astype(HALF)
    spectrum += jnp.dot(edges, edge_table[...], preferred_element_type=FLOAT)
    channel = lax.broadcasted_iota(jnp.int32, spectrum.shape, 0)
    spectrum = jnp.where(channel < dead[0], 0.0, spectrum)
    re, im = spectrum[:, :NF], spectrum[:, NF:]
    high, low = split(re * re + im * im)
    summed = jnp.dot(high, window[...], preferred_element_type=FLOAT)
    summed += jnp.dot(low, window[...], preferred_element_type=FLOAT)
    factor = lax.rsqrt(summed / counts[...] + 1e-05)
    re, im = re * factor, im * factor
    real[...] = re
    imag[...] = im
    white[:, :NF] = re.astype(HALF)
    white[:, NF:] = im.astype(HALF)


def whiten(pieces, dead, ordered):
    channels = pieces[0].shape[0] // 2 - EDGE
    blocks = 2 * len(pieces)
    window, counts = window_table()
    return pl.pallas_call(
        functools.partial(whiten_body, count=len(pieces), ordered=ordered),
        out_shape=(
            jax.ShapeDtypeStruct((channels, 2 * NF), HALF),
            jax.ShapeDtypeStruct((channels, NF), FLOAT),
            jax.ShapeDtypeStruct((channels, NF), FLOAT),
        ),
        in_specs=[pl.BlockSpec(memory_space=pltpu.SMEM)]
        + [pl.BlockSpec(memory_space=pltpu.VMEM)] * (4 + len(pieces)),
        out_specs=(pl.BlockSpec(memory_space=pltpu.VMEM),) * 3,
        scratch_shapes=[pltpu.VMEM((blocks * EDGE, LANES), FLOAT)],
        compiler_params=pltpu.CompilerParams(vmem_limit_bytes=24 << 20),
        name="whiten",
    )(
        dead,
        jnp.asarray(table_rows(np.arange(NT))),
        jnp.asarray(table_rows(edge_samples())),
        jnp.asarray(window),
        jnp.asarray(counts),
        *pieces,
    )


def send(value, shift, keep=lambda source: True):
    count = lax.axis_size("row")
    pairs = [(s, s - shift(s)) for s in range(count) if keep(s) and 0 <= s - shift(s) < count]
    return lax.ppermute(value, "row", pairs)


def beside(value, keep=lambda source: True):
    return send(value, lambda s: s - (s ^ 1), keep)


def gather_first(white):
    four = send(white, lambda s: 4)
    across = send(white, lambda s: s - (s ^ 2))
    return beside(white, lambda s: s % 2 == 1), four, across


def gather_second(four, across):
    six = send(four, lambda s: 2)
    two = send(across, lambda s: 4, lambda s: s & 2 == 2)
    return two, six, send(four, lambda s: 3, lambda s: s % 2 == 0)


WHOLE = pl.BlockSpec(memory_space=pltpu.VMEM)
SCALAR = pl.BlockSpec(memory_space=pltpu.SMEM)


def pair(left, columns, band, offset):
    product = lax.dot_general(
        left, columns, (((1,), (1,)), ((), ())), preferred_element_type=FLOAT
    )
    scale = jnp.where(offset < band[0], 1.0 / math.sqrt(NF), 0.0)
    return (product * scale).astype(HALF)


def by_parity(even, odd):
    return jnp.where(lax.axis_index("row") % 2 == 0, even, odd)


def cost(channels, tiles):
    return pl.CostEstimate(
        flops=2 * LAGS * tiles * channels * channels * 2 * NF,
        bytes_accessed=2 * LAGS * channels * (2 * NF + tiles * channels),
        transcendentals=0,
    )


def own_body(band, real, imag, cosine, sine, white, lagged, out):
    c, s = cosine[0], sine[0]
    re, im = real[...], imag[...]
    lagged[0, :, :NF] = (re * c - im * s).astype(HALF)
    lagged[0, :, NF:] = (re * s + im * c).astype(HALF)
    out[0] = pair(lagged[0], white[...], band, 0)


def correlate_own(band, real, imag, white):
    channels = real.shape[0]
    cosine, sine = lag_tables()
    return pl.pallas_call(
        own_body,
        out_shape=(
            jax.ShapeDtypeStruct((LAGS, channels, 2 * NF), HALF),
            jax.ShapeDtypeStruct((LAGS, channels, channels), HALF),
        ),
        grid=(LAGS,),
        in_specs=[
            SCALAR,
            WHOLE,
            WHOLE,
            pl.BlockSpec((1, 1, NF), lambda i: (i, 0, 0)),
            pl.BlockSpec((1, 1, NF), lambda i: (i, 0, 0)),
            WHOLE,
        ],
        out_specs=(
            pl.BlockSpec((1, channels, 2 * NF), lambda i: (i, 0, 0)),
            pl.BlockSpec((1, channels, channels), lambda i: (i, 0, 0)),
        ),
        compiler_params=pltpu.CompilerParams(vmem_limit_bytes=16 << 20),
        cost_estimate=cost(channels, 1),
        name="correlate_own",
    )(band, real, imag, jnp.asarray(cosine[:, None]), jnp.asarray(sine[:, None]), white)


def near_body(band, lagged, one, four, four_beside, seven, two, across, out, columns, sem):
    first = pl.program_id(0) == 0
    near_side = lax.axis_index("row") & 2 == 0
    pl.when(first & near_side)(pltpu.make_async_copy(across, columns, sem).start)
    pl.when(first & jnp.logical_not(near_side))(pltpu.make_async_copy(two, columns, sem).start)
    pl.when(first)(pltpu.make_async_copy(two, columns, sem).wait)
    group, channels = out.shape[1], out.shape[2]
    at = pl.ds(pl.program_id(0) * group, group)
    left = lagged[at].reshape(group * channels, 2 * NF)
    shape = (group, channels, channels)
    out[0] = pair(left, four[...], band, 4).reshape(shape)
    out[1] = pair(left, four_beside[...], band, by_parity(5, 3)).reshape(shape)
    out[2] = pair(left, one[...], band, 1).reshape(shape)
    out[3] = pair(left, seven[...], band, 7).reshape(shape)
    out[4] = pair(left, columns[...], band, 2).reshape(shape)


def correlate_near(band, lagged, *tiles):
    channels = lagged.shape[1]
    return pl.pallas_call(
        near_body,
        out_shape=jax.ShapeDtypeStruct((5, LAGS, channels, channels), HALF),
        grid=(LAGS // 2,),
        in_specs=[SCALAR] + [WHOLE] * 5 + [pl.BlockSpec(memory_space=pl.ANY)] * 2,
        out_specs=pl.BlockSpec((5, 2, channels, channels), lambda i: (0, i, 0, 0)),
        scratch_shapes=[pltpu.VMEM((channels, 2 * NF), HALF), pltpu.SemaphoreType.DMA],
        compiler_params=pltpu.CompilerParams(vmem_limit_bytes=24 << 20),
        cost_estimate=cost(channels, 5),
        name="correlate_near",
    )(band, lagged, *tiles)


EVEN = (0, 3, 5, 8, 1, 2, 6, 7)
ODD = (0, 8, 5, 2, 1, 7, 6, 4)


def far_body(
    band, lagged, own, near, six, six_beside, two_beside, across_beside, out, columns, sem,
    *, rows,
):
    step = pl.program_id(0)
    channels = six_beside.shape[0]
    first = step == 0
    near_side = lax.axis_index("row") & 2 == 0
    pl.when(first & near_side)(pltpu.make_async_copy(across_beside, columns, sem).start)
    pl.when(first & jnp.logical_not(near_side))(
        pltpu.make_async_copy(two_beside, columns, sem).start
    )
    pl.when(first)(pltpu.make_async_copy(two_beside, columns, sem).wait)

    def run(order, offsets):
        at = pl.ds(pl.multiple_of(step * rows, rows), rows)
        left = lagged[:, at, :].reshape(LAGS * rows, 2 * NF)
        far = [
            pair(left, tile, band, offset).reshape(LAGS, rows, channels)
            for tile, offset in zip((six[...], six_beside[...], columns[...]), offsets)
        ]
        for lag in range(LAGS):
            for half in range(channels // LANES):
                lanes = slice(half * LANES, (half + 1) * LANES)
                planes = []
                for plane in order:
                    if plane == 0:
                        planes.append(own[lag, at, lanes])
                    elif plane < 6:
                        planes.append(near[plane - 1, lag, at, lanes])
                    else:
                        planes.append(far[plane - 6][lag, :, lanes])
                out[:, lag, :, lanes] = pltpu.einshape("kab->akb", jnp.stack(planes))

    is_even = lax.axis_index("row") % 2 == 0
    pl.when(is_even)(lambda: run(EVEN, (6, 7, 3)))
    pl.when(jnp.logical_not(is_even))(lambda: run(ODD, (6, 5, 1)))


def correlate_far(band, lagged, own, near, *tiles):
    channels = lagged.shape[1]
    rows = 64
    return pl.pallas_call(
        functools.partial(far_body, rows=rows),
        out_shape=jax.ShapeDtypeStruct((channels, LAGS, NB, channels), HALF),
        grid=(channels // rows,),
        in_specs=[SCALAR] + [WHOLE] * 5 + [pl.BlockSpec(memory_space=pl.ANY)] * 2,
        out_specs=pl.BlockSpec((rows, LAGS, NB, channels), lambda i: (i, 0, 0, 0)),
        scratch_shapes=[pltpu.VMEM((channels, 2 * NF), HALF), pltpu.SemaphoreType.DMA],
        compiler_params=pltpu.CompilerParams(vmem_limit_bytes=32 << 20),
        cost_estimate=cost(channels, 3),
        name="correlate_far",
    )(band, lagged, own, near, *tiles)


def shards(raw, fir_taps, band_width, dead_count):
    tiles = lax.axis_size("row")
    if raw.shape[1] == DEC * LANES:
        white, real, imag = whiten(transpose_blocks(raw, fir_taps, tiles), dead_count, False)
    else:
        channel_block = lax.all_to_all(raw, "row", split_axis=0, concat_axis=1, tiled=True)
        white, real, imag = whiten(filter_whole(channel_block, fir_taps), dead_count, True)
    one, four, across = gather_first(white)
    lagged, own = correlate_own(band_width, real, imag, white)
    four, across, lagged = lax.optimization_barrier((four, across, lagged))
    one, lagged = lax.optimization_barrier((one, lagged))
    across, lagged = lax.optimization_barrier((across, lagged))
    two, six, seven = gather_second(four, across)
    across_beside = beside(across, lambda s: s & 2 == 0)
    four_beside = beside(four)
    near = correlate_near(band_width, lagged, one, four, four_beside, seven, two, across)
    two_beside = beside(two, lambda s: s & 2 == 2)
    six, near, two_beside = lax.optimization_barrier((six, near, two_beside))
    six_beside = beside(six)
    return correlate_far(band_width, lagged, own, near, six, six_beside, two_beside, across_beside)


def solution(mesh):
    return jax.shard_map(
        shards,
        mesh=mesh,
        in_specs=(P(None, ("win", "row")), P(), P("row"), P("row")),
        out_specs=P(("win", "row"), None, None, None),
        check_vma=False,
    )
```

```python
import functools
import math

import jax
import jax.numpy as jnp
import ml_dtypes
import numpy as np
from jax import lax
from jax.experimental import pallas as pl
from jax.experimental.pallas import tpu as pltpu
from jax.sharding import PartitionSpec as P

NT = 2048
NF = 512
DEC = 4
TAPS = 16
SMOOTH = 64
LAGS = 8
NB = 8
LEFT = (TAPS - DEC) // 2
LANES = 128
EDGE = 8
FLOAT = jnp.float32
HALF = jnp.bfloat16


def table_rows(samples):
    bins = np.arange(NF, dtype=np.int64)[None, :] + 1
    samples = np.asarray(samples, dtype=np.int64)[:, None]
    phases = (samples * bins % NT).astype(np.float64) * (2.0 * math.pi / NT)
    rows = np.concatenate([np.cos(phases), -np.sin(phases)], axis=1)
    inside = (samples >= 0) & (samples < NT)
    return np.where(inside, rows, 0.0).astype(ml_dtypes.bfloat16)


def edge_samples():
    blocks = NT // LANES
    offsets = np.array([-2, -1, LANES, LANES + 1] * 2)
    return (np.arange(blocks)[:, None] * LANES + offsets[None, :]).reshape(-1)


def window_table():
    ids = np.arange(NF)
    window = np.abs(ids[:, None] - ids[None, :]) <= SMOOTH
    counts = window.sum(axis=0).astype(np.float32)[None, :]
    return window.astype(ml_dtypes.bfloat16), counts


def lag_tables():
    lags = np.arange(LAGS, dtype=np.int64) - LAGS // 2
    bins = np.arange(NF, dtype=np.int64) + 1
    phases = ((lags % NT)[:, None] * bins[None, :] % NT) * (2.0 * math.pi / NT)
    return np.cos(phases).astype(np.float32), np.sin(phases).astype(np.float32)


def split(value):
    high = value.astype(HALF)
    low = (value - high.astype(FLOAT)).astype(HALF)
    return high, low


def spread_taps(taps, index):
    spread = jnp.zeros(index.shape, FLOAT)
    for tap in range(TAPS):
        spread = jnp.where(index == tap, taps[tap], spread)
    return spread


def filter_body(taps, raw, other, own, held, main, edge, sems, *, channels):
    width = raw.shape[1]
    step = pl.program_id(0)
    group = own.shape[0]
    count = held.shape[0] // 2
    chip = lax.axis_index("row") // 2
    parity = lax.axis_index("row") % 2

    @pl.when(step == 0)
    def _():
        for slot in range(2 * count):
            tile = (chip ^ (slot % count)) * 2 + (parity ^ (1 - slot // count))
            at = pl.ds(pl.multiple_of(tile * channels, channels), channels)
            pltpu.make_async_copy(raw.at[at], held.at[slot], sems.at[slot]).start()
        rows = lax.broadcasted_iota(jnp.int32, (width, LANES), 0)
        cols = lax.broadcasted_iota(jnp.int32, (width, LANES), 1)
        high, low = split(spread_taps(taps, rows - DEC * cols + LEFT))
        main[:, :LANES] = high
        main[:, LANES:] = low
        row = lax.broadcasted_iota(jnp.int32, (EDGE, 2 * LANES), 0) % 4
        lane = lax.broadcasted_iota(jnp.int32, (EDGE, 2 * LANES), 1)
        lane = jnp.where(lane < LANES, lane, lane + width - 2 * LANES)
        sample = jnp.where(row < 2, row - 2, row + LANES - 2)
        high, low = split(spread_taps(taps, lane - DEC * sample + LEFT))
        edge[...] = jnp.concatenate([high.astype(FLOAT), low.astype(FLOAT)], axis=0).astype(HALF)

    def run(out):
        slots = [step * group + index for index in range(group)]
        for slot in slots:
            pltpu.make_async_copy(raw.at[pl.ds(0, channels)], held.at[slot], sems.at[slot]).wait()
        for index, slot in enumerate(slots):
            block = held[slot]
            product = jnp.dot(block, main[...], preferred_element_type=FLOAT)
            out[index, :channels, :] = (product[:, :LANES] + product[:, LANES:]).astype(HALF)
            ends = jnp.concatenate([block[:, :LANES], block[:, width - LANES :]], axis=1)
            partial = lax.dot_general(
                edge[...], ends, (((1,), (1,)), ((), ())), preferred_element_type=FLOAT
            )
            partial = partial[:EDGE] + partial[EDGE:]
            row = lax.broadcasted_iota(jnp.int32, (EDGE, LANES), 0)
            picked = jnp.where(row < 4, partial[:, :LANES], partial[:, LANES:])
            out[index, channels:, :] = picked.astype(HALF)

    half = pl.num_programs(0) // 2
    pl.when(step < half)(lambda: run(other))
    pl.when(step >= half)(lambda: run(own))


def filter_blocks(raw, fir_taps, tiles):
    channels = raw.shape[0] // tiles
    width = raw.shape[1]
    chips = tiles // 2
    group = 4
    half = chips // group
    block = (group, channels + EDGE, LANES)
    return pl.pallas_call(
        functools.partial(filter_body, channels=channels),
        out_shape=(jax.ShapeDtypeStruct((chips, channels + EDGE, LANES), HALF),) * 2,
        grid=(2 * half,),
        in_specs=[
            pl.BlockSpec(memory_space=pltpu.SMEM),
            pl.BlockSpec(memory_space=pl.ANY),
        ],
        out_specs=(
            pl.BlockSpec(block, lambda i: (jnp.minimum(i, half - 1), 0, 0)),
            pl.BlockSpec(block, lambda i: (jnp.maximum(i - half, 0), 0, 0)),
        ),
        scratch_shapes=[
            pltpu.VMEM((tiles, channels, width), HALF),
            pltpu.VMEM((width, 2 * LANES), HALF),
            pltpu.VMEM((2 * EDGE, 2 * LANES), HALF),
            pltpu.SemaphoreType.DMA((tiles,)),
        ],
        compiler_params=pltpu.CompilerParams(vmem_limit_bytes=58 << 20),
        name="filter",
    )(fir_taps, raw)


def transpose_blocks(raw, fir_taps, tiles):
    other, own = filter_blocks(raw, fir_taps, tiles)
    came = lax.ppermute(other, "row", [(s, s ^ 1) for s in range(tiles)])
    pieces = [jnp.concatenate([own[d], came[d]], axis=0) for d in range(tiles // 2)]
    pieces = lax.optimization_barrier(pieces)
    return pieces[:1] + [
        lax.ppermute(pieces[d], "row", [(s, s ^ (2 * d)) for s in range(tiles)])
        for d in range(1, tiles // 2)
    ]


def filter_whole(channel_block, fir_taps):
    padded = jnp.pad(channel_block.astype(FLOAT), ((0, 0), (2 * DEC, 2 * DEC)))
    rows = padded.shape[0]
    phased = jnp.transpose(padded.reshape(rows, -1, DEC), (2, 0, 1))
    filtered = jnp.zeros((rows, NT), FLOAT)
    for tap in range(TAPS):
        first_at = 2 * DEC - LEFT + tap
        begin = first_at // DEC
        filtered = filtered + fir_taps[tap] * phased[first_at % DEC, :, begin : begin + NT]
    blocks = filtered.astype(HALF).reshape(rows, NT // LANES, LANES).transpose(1, 0, 2)
    blocks = jnp.concatenate([blocks, jnp.zeros((NT // LANES, EDGE, LANES), HALF)], axis=1)
    return [blocks[d : d + 2].reshape(-1, LANES) for d in range(0, NT // LANES, 2)]


def whiten_body(dead, table, edge_table, window, counts, *rest, count, ordered):
    pieces, white, real, imag, ends = rest[:count], *rest[count:]
    channels = white.shape[0]
    height = channels + EDGE
    chip = 0 if ordered else lax.axis_index("row") // 2
    parity = 0 if ordered else lax.axis_index("row") % 2

    spectrum = jnp.zeros((channels, 2 * NF), FLOAT)
    for index, piece in enumerate(pieces):
        source = index if ordered else chip ^ index
        mine, other = piece[:channels, :], piece[height : height + channels, :]
        if ordered:
            left = jnp.concatenate([mine, other], axis=1)
        else:
            left = jnp.concatenate(
                [jnp.where(parity == 0, mine, other), jnp.where(parity == 0, other, mine)], axis=1
            )
        for part in range(2):
            block = source * 2 + (part if ordered else part ^ parity)
            at = pl.ds(pl.multiple_of(block * EDGE, EDGE), EDGE)
            ends[at, :] = piece[part * height + channels : (part + 1) * height, :].astype(FLOAT)
        at = pl.ds(pl.multiple_of(source * (2 * LANES), 2 * LANES), 2 * LANES)
        spectrum += jnp.dot(left, table[at, :], preferred_element_type=FLOAT)

    turned = ends[...].T
    lane = lax.broadcasted_iota(jnp.int32, turned.shape, 1) % EDGE
    first = jnp.where(lane < 4, turned, 0.0)
    second = jnp.where(lane < 4, 0.0, turned)
    edges = jnp.concatenate([first, second], axis=0).astype(HALF)
    spectrum += jnp.dot(edges, edge_table[...], preferred_element_type=FLOAT)
    channel = lax.broadcasted_iota(jnp.int32, spectrum.shape, 0)
    spectrum = jnp.where(channel < dead[0], 0.0, spectrum)
    re, im = spectrum[:, :NF], spectrum[:, NF:]
    high, low = split(re * re + im * im)
    summed = jnp.dot(high, window[...], preferred_element_type=FLOAT)
    summed += jnp.dot(low, window[...], preferred_element_type=FLOAT)
    factor = lax.rsqrt(summed / counts[...] + 1e-05)
    re, im = re * factor, im * factor
    real[...] = re
    imag[...] = im
    white[:, :NF] = re.astype(HALF)
    white[:, NF:] = im.astype(HALF)


def whiten(pieces, dead, ordered):
    channels = pieces[0].shape[0] // 2 - EDGE
    blocks = 2 * len(pieces)
    window, counts = window_table()
    return pl.pallas_call(
        functools.partial(whiten_body, count=len(pieces), ordered=ordered),
        out_shape=(
            jax.ShapeDtypeStruct((channels, 2 * NF), HALF),
            jax.ShapeDtypeStruct((channels, NF), FLOAT),
            jax.ShapeDtypeStruct((channels, NF), FLOAT),
        ),
        in_specs=[pl.BlockSpec(memory_space=pltpu.SMEM)]
        + [pl.BlockSpec(memory_space=pltpu.VMEM)] * (4 + len(pieces)),
        out_specs=(pl.BlockSpec(memory_space=pltpu.VMEM),) * 3,
        scratch_shapes=[pltpu.VMEM((blocks * EDGE, LANES), FLOAT)],
        compiler_params=pltpu.CompilerParams(vmem_limit_bytes=24 << 20),
        name="whiten",
    )(
        dead,
        jnp.asarray(table_rows(np.arange(NT))),
        jnp.asarray(table_rows(edge_samples())),
        jnp.asarray(window),
        jnp.asarray(counts),
        *pieces,
    )


def send(value, shift, keep=lambda source: True):
    count = lax.axis_size("row")
    pairs = [(s, s - shift(s)) for s in range(count) if keep(s) and 0 <= s - shift(s) < count]
    return lax.ppermute(value, "row", pairs)


def beside(value, keep=lambda source: True):
    return send(value, lambda s: s - (s ^ 1), keep)


def gather_first(white):
    four = send(white, lambda s: 4)
    across = send(white, lambda s: s - (s ^ 2))
    return beside(white, lambda s: s % 2 == 1), four, across


def gather_second(four, across):
    six = send(four, lambda s: 2)
    two = send(across, lambda s: 4, lambda s: s & 2 == 2)
    return two, six, send(four, lambda s: 3, lambda s: s % 2 == 0)


WHOLE = pl.BlockSpec(memory_space=pltpu.VMEM)
SCALAR = pl.BlockSpec(memory_space=pltpu.SMEM)


def pair(left, columns, band, offset):
    product = lax.dot_general(
        left, columns, (((1,), (1,)), ((), ())), preferred_element_type=FLOAT
    )
    scale = jnp.where(offset < band[0], 1.0 / math.sqrt(NF), 0.0)
    return (product * scale).astype(HALF)


def by_parity(even, odd):
    return jnp.where(lax.axis_index("row") % 2 == 0, even, odd)


def cost(channels, tiles):
    return pl.CostEstimate(
        flops=2 * LAGS * tiles * channels * channels * 2 * NF,
        bytes_accessed=2 * LAGS * channels * (2 * NF + tiles * channels),
        transcendentals=0,
    )


def own_body(band, real, imag, cosine, sine, white, lagged, out):
    c, s = cosine[0], sine[0]
    re, im = real[...], imag[...]
    lagged[0, :, :NF] = (re * c - im * s).astype(HALF)
    lagged[0, :, NF:] = (re * s + im * c).astype(HALF)
    out[0] = pair(lagged[0], white[...], band, 0)


def correlate_own(band, real, imag, white):
    channels = real.shape[0]
    cosine, sine = lag_tables()
    return pl.pallas_call(
        own_body,
        out_shape=(
            jax.ShapeDtypeStruct((LAGS, channels, 2 * NF), HALF),
            jax.ShapeDtypeStruct((LAGS, channels, channels), HALF),
        ),
        grid=(LAGS,),
        in_specs=[
            SCALAR,
            WHOLE,
            WHOLE,
            pl.BlockSpec((1, 1, NF), lambda i: (i, 0, 0)),
            pl.BlockSpec((1, 1, NF), lambda i: (i, 0, 0)),
            WHOLE,
        ],
        out_specs=(
            pl.BlockSpec((1, channels, 2 * NF), lambda i: (i, 0, 0)),
            pl.BlockSpec((1, channels, channels), lambda i: (i, 0, 0)),
        ),
        compiler_params=pltpu.CompilerParams(vmem_limit_bytes=16 << 20),
        cost_estimate=cost(channels, 1),
        name="correlate_own",
    )(band, real, imag, jnp.asarray(cosine[:, None]), jnp.asarray(sine[:, None]), white)


def near_body(band, lagged, one, four, four_beside, seven, two, across, out, columns, sem):
    first = pl.program_id(0) == 0
    near_side = lax.axis_index("row") & 2 == 0
    pl.when(first & near_side)(pltpu.make_async_copy(across, columns, sem).start)
    pl.when(first & jnp.logical_not(near_side))(pltpu.make_async_copy(two, columns, sem).start)
    pl.when(first)(pltpu.make_async_copy(two, columns, sem).wait)
    group, channels = out.shape[1], out.shape[2]
    at = pl.ds(pl.program_id(0) * group, group)
    left = lagged[at].reshape(group * channels, 2 * NF)
    shape = (group, channels, channels)
    out[0] = pair(left, four[...], band, 4).reshape(shape)
    out[1] = pair(left, four_beside[...], band, by_parity(5, 3)).reshape(shape)
    out[2] = pair(left, one[...], band, 1).reshape(shape)
    out[3] = pair(left, seven[...], band, 7).reshape(shape)
    out[4] = pair(left, columns[...], band, 2).reshape(shape)


def correlate_near(band, lagged, *tiles):
    channels = lagged.shape[1]
    return pl.pallas_call(
        near_body,
        out_shape=jax.ShapeDtypeStruct((5, LAGS, channels, channels), HALF),
        grid=(LAGS // 4,),
        in_specs=[SCALAR] + [WHOLE] * 5 + [pl.BlockSpec(memory_space=pl.ANY)] * 2,
        out_specs=pl.BlockSpec((5, 4, channels, channels), lambda i: (0, i, 0, 0)),
        scratch_shapes=[pltpu.VMEM((channels, 2 * NF), HALF), pltpu.SemaphoreType.DMA],
        compiler_params=pltpu.CompilerParams(vmem_limit_bytes=24 << 20),
        cost_estimate=cost(channels, 5),
        name="correlate_near",
    )(band, lagged, *tiles)


EVEN = (0, 3, 5, 8, 1, 2, 6, 7)
ODD = (0, 8, 5, 2, 1, 7, 6, 4)


def far_body(
    band, lagged, own, near, six, six_beside, two_beside, across_beside, out, columns, sem,
    *, rows,
):
    step = pl.program_id(0)
    channels = six_beside.shape[0]
    first = step == 0
    near_side = lax.axis_index("row") & 2 == 0
    pl.when(first & near_side)(pltpu.make_async_copy(across_beside, columns, sem).start)
    pl.when(first & jnp.logical_not(near_side))(
        pltpu.make_async_copy(two_beside, columns, sem).start
    )
    pl.when(first)(pltpu.make_async_copy(two_beside, columns, sem).wait)

    def run(order, offsets):
        at = pl.ds(pl.multiple_of(step * rows, rows), rows)
        left = lagged[:, at, :].reshape(LAGS * rows, 2 * NF)
        far = [
            pair(left, tile, band, offset).reshape(LAGS, rows, channels)
            for tile, offset in zip((six[...], six_beside[...], columns[...]), offsets)
        ]
        for lag in range(LAGS):
            for half in range(channels // LANES):
                lanes = slice(half * LANES, (half + 1) * LANES)
                planes = []
                for plane in order:
                    if plane == 0:
                        planes.append(own[lag, at, lanes])
                    elif plane < 6:
                        planes.append(near[plane - 1, lag, at, lanes])
                    else:
                        planes.append(far[plane - 6][lag, :, lanes])
                out[:, lag, :, lanes] = pltpu.einshape("kab->akb", jnp.stack(planes))

    is_even = lax.axis_index("row") % 2 == 0
    pl.when(is_even)(lambda: run(EVEN, (6, 7, 3)))
    pl.when(jnp.logical_not(is_even))(lambda: run(ODD, (6, 5, 1)))


def correlate_far(band, lagged, own, near, *tiles):
    channels = lagged.shape[1]
    rows = 64
    return pl.pallas_call(
        functools.partial(far_body, rows=rows),
        out_shape=jax.ShapeDtypeStruct((channels, LAGS, NB, channels), HALF),
        grid=(channels // rows,),
        in_specs=[SCALAR] + [WHOLE] * 5 + [pl.BlockSpec(memory_space=pl.ANY)] * 2,
        out_specs=pl.BlockSpec((rows, LAGS, NB, channels), lambda i: (i, 0, 0, 0)),
        scratch_shapes=[pltpu.VMEM((channels, 2 * NF), HALF), pltpu.SemaphoreType.DMA],
        compiler_params=pltpu.CompilerParams(vmem_limit_bytes=32 << 20),
        cost_estimate=cost(channels, 3),
        name="correlate_far",
    )(band, lagged, own, near, *tiles)


def shards(raw, fir_taps, band_width, dead_count):
    tiles = lax.axis_size("row")
    if raw.shape[1] == DEC * LANES:
        white, real, imag = whiten(transpose_blocks(raw, fir_taps, tiles), dead_count, False)
    else:
        channel_block = lax.all_to_all(raw, "row", split_axis=0, concat_axis=1, tiled=True)
        white, real, imag = whiten(filter_whole(channel_block, fir_taps), dead_count, True)
    one, four, across = gather_first(white)
    lagged, own = correlate_own(band_width, real, imag, white)
    four, across, lagged = lax.optimization_barrier((four, across, lagged))
    one, lagged = lax.optimization_barrier((one, lagged))
    across, lagged = lax.optimization_barrier((across, lagged))
    two, six, seven = gather_second(four, across)
    across_beside = beside(across, lambda s: s & 2 == 0)
    four_beside = beside(four)
    near = correlate_near(band_width, lagged, one, four, four_beside, seven, two, across)
    two_beside = beside(two, lambda s: s & 2 == 2)
    six, near, two_beside = lax.optimization_barrier((six, near, two_beside))
    six_beside = beside(six)
    return correlate_far(band_width, lagged, own, near, six, six_beside, two_beside, across_beside)


def solution(mesh):
    return jax.shard_map(
        shards,
        mesh=mesh,
        in_specs=(P(None, ("win", "row")), P(), P("row"), P("row")),
        out_specs=P(("win", "row"), None, None, None),
        check_vma=False,
    )
```
